256 devices in a mesh: group: 2 (over z_lo), inner: 128 (over x, z_hi, y, core).
Axes of the slice: x: 4, y: 4, z: 8 (z_hi: 4, z_lo: 2; z = z_hi * 2 + z_lo), core: 2. Of those that a mesh axis runs over, the one named last changes fastest.
Arguments:
- voltages: bfloat16 [128, 768, 2, 16, 128], P('inner', 'group'), may hold values from -7 to 7
- coeffs: float32 [3, 16, 128], replicated, may hold values from -2 to 2
Outputs:
- autos: float32 [128, 2, 768, 384], P('inner', None, 'group')
- cross: float32 [128, 2, 384, 384], P('inner', None, 'group')
The draws below stay inside these ranges and needn't reach their ends.
All inputs are finite; a program needn't handle non-finite values.
Results may differ from the reference program's by a relative error of at most 0.0025.
Values may be sent and summed in bfloat16 or wider, within the bound.
A program may use at most 320 MiB of HBM per device.

```python
import math
import jax
import jax.numpy as jnp
import numpy as np
from jax import lax

SUBCHANNELS = 16
TAPS = 3
CHANNELS = 128
INPUTS = 768
IN_G = 384
FRAMES = 128


def draw_voltages(key, part):
    shape_full = (FRAMES, INPUTS, 2, SUBCHANNELS, CHANNELS)
    shape_common = (FRAMES, 1, 2, SUBCHANNELS, CHANNELS)
    key_common = jax.random.fold_in(key, 11)
    key_noise = jax.random.fold_in(key, 12)
    key_amplitude = jax.random.fold_in(key, 13)
    key_phase = jax.random.fold_in(key, 14)
    common = 0.7 * jax.random.truncated_normal(key_common, -4.0, 4.0, shape_common, jnp.float32)
    noise = 0.7 * jax.random.truncated_normal(key_noise, -4.0, 4.0, shape_full, jnp.float32)
    amplitude = jax.random.uniform(key_amplitude, (1, INPUTS, 1, 1, 1), jnp.float32, 0.3, 1.0)
    phase = jax.random.uniform(key_phase, (1, INPUTS, 1, 1, 1), jnp.float32, -math.pi, math.pi)
    cos_phase = jnp.cos(phase)
    sin_phase = jnp.sin(phase)
    common_real = common[:, :, 0:1]
    common_imag = common[:, :, 1:2]
    rotated_real = cos_phase * common_real - sin_phase * common_imag
    rotated_imag = sin_phase * common_real + cos_phase * common_imag
    rotated = jnp.concatenate([rotated_real, rotated_imag], axis=2)
    return (amplitude * rotated + noise).astype(jnp.bfloat16)


def normal_values(key, dims, spread, bound, held_as=jnp.bfloat16):
    return jnp.clip(spread * jax.random.normal(key, dims, jnp.float32), -bound, bound).astype(held_as)


def setup_inputs(seed: int = 0) -> dict:
    keys = jax.random.split(jax.random.key(seed), 3)
    return {
        "voltages": draw_voltages(jax.random.fold_in(keys[2], 71), 0),
        "coeffs": normal_values(keys[1], (TAPS, SUBCHANNELS, CHANNELS), 0.41, 2.0, jnp.float32),
    }


def dft_block(length_dft):
    indices = np.arange(length_dft)
    angles = 2.0 * np.pi * (indices[:, None] * indices[None, :] % length_dft) / length_dft
    cosine = np.cos(angles)
    sine_table = np.sin(angles)
    upper = np.stack([cosine, -sine_table], axis=1)
    lower = np.stack([sine_table, cosine], axis=1)
    return np.stack([upper, lower], axis=0)

def twiddle_tables():
    fine_count = SUBCHANNELS * CHANNELS
    rows_k = np.arange(SUBCHANNELS)[:, None]
    cols_q = np.arange(CHANNELS)[None, :]
    angles = 2.0 * np.pi * (rows_k * cols_q % fine_count) / fine_count
    factor = 1.0 / math.sqrt(fine_count)
    return (np.cos(angles) * factor, np.sin(angles) * factor)

def filterbank_ref(extended, coeffs, frame_count):
    history_len = TAPS - 1
    accumulated = jnp.zeros((frame_count,) + extended.shape[1:], jnp.float32)
    for tap_index in range(TAPS):
        window = extended[history_len - tap_index:history_len - tap_index + frame_count].astype(jnp.float32)
        accumulated = accumulated + coeffs[tap_index] * window
    filtered = accumulated.astype(jnp.bfloat16)
    inputs_count = filtered.shape[1]
    flat_in = filtered.reshape(frame_count, inputs_count, 2 * SUBCHANNELS, CHANNELS).astype(jnp.float32)
    first_table = jnp.asarray(dft_block(SUBCHANNELS).reshape(2 * SUBCHANNELS, 2 * SUBCHANNELS), jnp.float32)
    first_table = first_table.astype(jnp.bfloat16).astype(jnp.float32)
    section_one = jnp.einsum('fixq,xy->fiyq', flat_in, first_table, precision=lax.Precision.HIGHEST)
    section_one = section_one.reshape(frame_count, inputs_count, 2, SUBCHANNELS, CHANNELS)
    real_part = section_one[:, :, 0]
    imag_part = section_one[:, :, 1]
    cos_np, sin_np = twiddle_tables()
    cosine_tw = jnp.asarray(cos_np, jnp.float32)
    sine_tw = jnp.asarray(sin_np, jnp.float32)
    tw_real = real_part * cosine_tw + imag_part * sine_tw
    tw_imag = imag_part * cosine_tw - real_part * sine_tw
    twisted = jnp.stack([tw_real, tw_imag], axis=3).astype(jnp.bfloat16)
    twisted = twisted.reshape(frame_count, inputs_count, SUBCHANNELS, 2 * CHANNELS).astype(jnp.float32)
    second_table = jnp.asarray(dft_block(CHANNELS).reshape(2 * CHANNELS, 2, CHANNELS), jnp.float32)
    second_table = second_table.astype(jnp.bfloat16).astype(jnp.float32)
    spectra = jnp.einsum('fiks,srm->mfkri', twisted, second_table, precision=lax.Precision.HIGHEST)
    return spectra.astype(jnp.bfloat16)

def reference(voltages, coeffs):
    history_len = TAPS - 1
    span_size = min(32, INPUTS)
    block_count = INPUTS // span_size
    padded = jnp.concatenate([jnp.zeros((history_len,) + voltages.shape[1:], voltages.dtype), voltages], 0)
    pieces = padded.reshape(FRAMES + history_len, block_count, span_size, 2, SUBCHANNELS, CHANNELS)
    pieces = pieces.transpose(1, 0, 2, 3, 4, 5)
    spectra = lax.map(lambda block_piece: filterbank_ref(block_piece, coeffs, FRAMES), pieces)
    spectra = spectra.transpose(1, 2, 3, 4, 0, 5).reshape(CHANNELS, FRAMES, SUBCHANNELS, 2, INPUTS)
    scale_factor = 1.0 / (FRAMES * SUBCHANNELS)

    def correlate(channel_data):
        values = channel_data.astype(jnp.float32)
        flipped = jnp.stack([values[:, :, 1], -values[:, :, 0]], axis=2)
        stacked = jnp.stack([values, flipped], 0).reshape(2, -1, INPUTS)
        flat_values = values.reshape(-1, INPUTS)
        auto_zero = jnp.einsum('rsa,sb->rab', stacked[:, :, :IN_G], flat_values[:, :IN_G], precision=lax.Precision.HIGHEST)
        auto_one = jnp.einsum('rsa,sb->rab', stacked[:, :, IN_G:], flat_values[:, IN_G:], precision=lax.Precision.HIGHEST)
        cross_block = jnp.einsum('rsa,sb->rab', stacked[:, :, IN_G:], flat_values[:, :IN_G], precision=lax.Precision.HIGHEST)
        return (jnp.concatenate([auto_zero, auto_one], 1) * scale_factor, cross_block * scale_factor)
    autos, cross = lax.map(correlate, spectra)
    return (autos, cross)
```

```python
import functools
import math

import jax
import jax.numpy as jnp
import numpy as np
from jax import lax
from jax.experimental import pallas as pl
from jax.experimental.pallas import tpu as pltpu
from jax.sharding import PartitionSpec as P

MESH_ID = pl.DeviceIdType.MESH

SUBCHANNELS = 16
TAPS = 3


def passed_along(x, axis, by):
    devices = lax.axis_size(axis)
    pairs = [(i, i + by) for i in range(devices) if 0 <= i + by < devices]
    return lax.ppermute(x, axis, pairs)


def partner(x, axis, distance):
    return lax.ppermute(x, axis, [(i, i ^ 1 << distance) for i in range(lax.axis_size(axis))])


def dft_block(length_dft):
    indices = np.arange(length_dft)
    angles = 2.0 * np.pi * (indices[:, None] * indices[None, :] % length_dft) / length_dft
    cosine = np.cos(angles)
    sine_table = np.sin(angles)
    upper = np.stack([cosine, -sine_table], axis=1)
    lower = np.stack([sine_table, cosine], axis=1)
    return np.stack([upper, lower], axis=0)


def twiddle_tables(channel_count):
    fine_count = SUBCHANNELS * channel_count
    rows_k = np.arange(SUBCHANNELS)[:, None]
    cols_q = np.arange(channel_count)[None, :]
    angles = 2.0 * np.pi * (rows_k * cols_q % fine_count) / fine_count
    factor = 1.0 / math.sqrt(fine_count)
    return (np.cos(angles) * factor, np.sin(angles) * factor)


def filterbank(extended, coeffs, frame_count):
    history_len = TAPS - 1
    channel_count = extended.shape[-1]
    accumulated = jnp.zeros((frame_count,) + extended.shape[1:], jnp.float32)
    for tap_index in range(TAPS):
        window = extended[history_len - tap_index : history_len - tap_index + frame_count].astype(
            jnp.float32
        )
        accumulated = accumulated + coeffs[tap_index] * window
    filtered = accumulated.astype(jnp.bfloat16)
    inputs_count = filtered.shape[1]
    flat_in = filtered.reshape(frame_count, inputs_count, 2 * SUBCHANNELS, channel_count)
    first_table = jnp.asarray(
        dft_block(SUBCHANNELS).reshape(2 * SUBCHANNELS, 2 * SUBCHANNELS), jnp.float32
    ).astype(jnp.bfloat16)
    section_one = jnp.einsum(
        "fixq,xy->fiyq", flat_in, first_table, preferred_element_type=jnp.float32
    )
    section_one = section_one.reshape(frame_count, inputs_count, 2, SUBCHANNELS, channel_count)
    real_part = section_one[:, :, 0]
    imag_part = section_one[:, :, 1]
    cos_np, sin_np = twiddle_tables(channel_count)
    cosine_tw = jnp.asarray(cos_np, jnp.float32)
    sine_tw = jnp.asarray(sin_np, jnp.float32)
    tw_real = real_part * cosine_tw + imag_part * sine_tw
    tw_imag = imag_part * cosine_tw - real_part * sine_tw
    twisted = jnp.stack([tw_real, tw_imag], axis=3).astype(jnp.bfloat16)
    twisted = twisted.reshape(frame_count, inputs_count, SUBCHANNELS, 2 * channel_count)
    second_table = jnp.asarray(
        dft_block(channel_count).reshape(2 * channel_count, 2, channel_count), jnp.float32
    ).astype(jnp.bfloat16)
    spectra = jnp.einsum(
        "fiks,srm->mfkri", twisted, second_table, preferred_element_type=jnp.float32
    )
    return spectra.astype(jnp.bfloat16)


def correlate_block(row_source, column_source):
    flipped = jnp.stack([row_source[:, :, :, 1], -row_source[:, :, :, 0]], axis=3)
    chan_count = row_source.shape[0]
    stacked = jnp.stack([row_source, flipped], 1).reshape(chan_count, 2, -1, row_source.shape[4])
    flat_columns = column_source.reshape(chan_count, -1, column_source.shape[4])
    return jnp.einsum("crsa,csb->crab", stacked, flat_columns, preferred_element_type=jnp.float32)


def turn_kernel(count, src, dst, send_sem, recv_sem, own_sem):
    me = lax.axis_index("inner")
    barrier = pltpu.get_barrier_semaphore()

    def greet(step, carry):
        pl.semaphore_signal(
            barrier, inc=1, device_id={"inner": lax.rem(me + step, count)}, device_id_type=MESH_ID
        )
        return carry

    lax.fori_loop(1, count, greet, 0)
    own = pltpu.make_async_copy(src.at[me], dst.at[me], own_sem)
    own.start()
    pl.semaphore_wait(barrier, count - 1)

    def send(step, carry):
        peer = lax.rem(me + step, count)
        pltpu.make_async_remote_copy(
            src_ref=src.at[peer],
            dst_ref=dst.at[me],
            send_sem=send_sem,
            recv_sem=recv_sem,
            device_id={"inner": peer},
            device_id_type=MESH_ID,
        ).start()
        return carry

    lax.fori_loop(1, count, send, 0)
    own.wait()
    rest = pl.ds(0, count - 1)
    pltpu.make_async_copy(src.at[rest], dst.at[rest], send_sem).wait()
    pltpu.make_async_copy(src.at[rest], dst.at[rest], recv_sem).wait()


def corner_turn(spectra):
    count = spectra.shape[0]
    return pl.pallas_call(
        functools.partial(turn_kernel, count),
        out_shape=jax.ShapeDtypeStruct(spectra.shape, spectra.dtype),
        in_specs=[pl.BlockSpec(memory_space=pltpu.VMEM)],
        out_specs=pl.BlockSpec(memory_space=pltpu.VMEM),
        scratch_shapes=[pltpu.SemaphoreType.DMA] * 3,
        compiler_params=pltpu.CompilerParams(collective_id=0, has_side_effects=True),
    )(spectra)


def shards(voltages, coeffs):
    history_len = TAPS - 1
    frame_count = voltages.shape[0]
    distances = (history_len + frame_count - 1) // frame_count
    received = []
    for distance in range(1, distances + 1):
        wanted = min(frame_count, history_len - (distance - 1) * frame_count)
        received.append(passed_along(voltages, "inner", distance))
    extended = jnp.concatenate(received[::-1] + [voltages], 0)
    spectra = filterbank(extended, coeffs, frame_count)
    chan_count = spectra.shape[0]
    rows = spectra.reshape(chan_count, 2 * SUBCHANNELS * frame_count, spectra.shape[-1])
    turned = corner_turn(rows).reshape(1, chan_count * frame_count, SUBCHANNELS, 2, -1)
    total_frames = turned.shape[1]
    scale_factor = 1.0 / (total_frames * SUBCHANNELS)
    autos = correlate_block(turned, turned) * scale_factor
    group_index = lax.axis_index("group")
    half_frames = total_frames // 2
    mine_half = lax.dynamic_slice_in_dim(turned, group_index * half_frames, half_frames, axis=1)
    send_half = lax.dynamic_slice_in_dim(
        turned, (1 - group_index) * half_frames, half_frames, axis=1
    )
    incoming = partner(send_half, "group", 0)
    row_source = jnp.where(group_index == 1, mine_half, incoming)
    column_source = jnp.where(group_index == 0, mine_half, incoming)
    partial_value = correlate_block(row_source, column_source) * scale_factor
    cross = lax.psum_scatter(partial_value, "group", scatter_dimension=2, tiled=True)
    return (autos, cross)


def solution(mesh):
    placed = (P("inner", "group", None, None, None), P())
    return jax.shard_map(
        shards,
        mesh=mesh,
        in_specs=placed,
        out_specs=(P("inner", None, "group", None), P("inner", None, "group", None)),
        check_vma=False,
    )
```

```python
import functools
import math

import jax
import jax.numpy as jnp
import numpy as np
from jax import lax
from jax.experimental import pallas as pl
from jax.experimental.pallas import tpu as pltpu
from jax.sharding import PartitionSpec as P

MESH_ID = pl.DeviceIdType.MESH
SUBCHANNELS = 16
TAPS = 3
CHANNELS = 128
RING = 8
BLOCKS = 16
ZS = 4
XS = 4
HISTORY = TAPS - 1
LANES = 128
CHUNK = 16


def dft_block(length_dft):
    indices = np.arange(length_dft)
    angles = 2.0 * np.pi * (indices[:, None] * indices[None, :] % length_dft) / length_dft
    cosine = np.cos(angles)
    sine_table = np.sin(angles)
    upper = np.stack([cosine, -sine_table], axis=1)
    lower = np.stack([sine_table, cosine], axis=1)
    return np.stack([upper, lower], axis=0)


def twiddle_tables(channel_count):
    fine_count = SUBCHANNELS * channel_count
    rows_k = np.arange(SUBCHANNELS)[:, None]
    cols_q = np.arange(channel_count)[None, :]
    angles = 2.0 * np.pi * (rows_k * cols_q % fine_count) / fine_count
    factor = 1.0 / math.sqrt(fine_count)
    return (np.cos(angles) * factor, np.sin(angles) * factor)


def tables():
    small = dft_block(SUBCHANNELS)
    first = np.einsum("fg,rpsk->sfkgrp", np.eye(RING), small)
    rows = RING * 2 * SUBCHANNELS
    first = first.reshape(rows, rows)
    second = dft_block(CHANNELS).reshape(2 * CHANNELS, 2 * CHANNELS).T
    order = np.einsum("ij,mn->mijn", np.eye(CHUNK), np.eye(CHUNK))
    order = order.reshape(CHUNK * CHUNK, CHUNK * CHUNK)
    cos_np, sin_np = twiddle_tables(CHANNELS)
    as_bf16 = [jnp.asarray(t, jnp.float32).astype(jnp.bfloat16) for t in (first, second, order)]
    as_f32 = [jnp.asarray(np.tile(t, (RING, 1)), jnp.float32) for t in (cos_np, sin_np)]
    return as_bf16 + as_f32


def ring_turn_kernel(per, volts, out, send_sem, recv_sem, halo_send, halo_recv):
    me = lax.axis_index("inner")
    count = lax.axis_size("inner")
    ring = lax.rem(me, RING)
    base = me - ring
    following = lax.rem(me + RING, count)
    previous = lax.rem(me + count - RING, count)
    tail = ring // (RING - HISTORY)
    chunks = per // CHUNK
    barrier = pltpu.get_barrier_semaphore()
    peers = [base + lax.rem(ring + s, RING) for s in range(1, RING)]
    for peer in peers + [following, previous]:
        pl.semaphore_signal(barrier, inc=1, device_id={"inner": peer}, device_id_type=MESH_ID)
    pl.semaphore_wait(barrier, RING + 1)
    for k in range(chunks):
        part = pl.ds(k * CHUNK, CHUNK)
        for s in range(1, RING):
            owner = lax.rem(ring + s, RING)
            pltpu.make_async_remote_copy(
                src_ref=volts.at[pl.ds(owner * per + k * CHUNK, CHUNK)],
                dst_ref=out.at[HISTORY + ring, part],
                send_sem=send_sem,
                recv_sem=recv_sem.at[k, tail],
                device_id={"inner": base + owner},
                device_id_type=MESH_ID,
            ).start()
        pltpu.make_async_copy(
            volts.at[pl.ds(ring * per + k * CHUNK, CHUNK)],
            out.at[HISTORY + ring, part],
            recv_sem.at[k, tail],
        ).start()
    for k in range(chunks):
        part = pl.ds(k * CHUNK, CHUNK)
        last = out.at[pl.ds(RING, HISTORY), part]
        first = out.at[pl.ds(0, HISTORY), part]
        pltpu.make_async_copy(last, last, recv_sem.at[k, 1]).wait()
        pltpu.make_async_remote_copy(
            src_ref=last,
            dst_ref=first,
            send_sem=halo_send,
            recv_sem=halo_recv.at[k],
            device_id={"inner": following},
            device_id_type=MESH_ID,
        ).start()
    for k in range(chunks):
        part = pl.ds(k * CHUNK, CHUNK)
        early = out.at[pl.ds(HISTORY, RING - HISTORY), part]
        pltpu.make_async_copy(early, early, recv_sem.at[k, 0]).wait()
        first = out.at[pl.ds(0, HISTORY), part]
        pltpu.make_async_copy(first, first, halo_recv.at[k]).wait()
    sent = volts.at[pl.ds(0, (RING - 1) * per)]
    pltpu.make_async_copy(sent, sent, send_sem).wait()
    first = out.at[pl.ds(0, HISTORY)]
    pltpu.make_async_copy(first, first, halo_send).wait()

    @pl.when(me < RING)
    def _():
        out[0:HISTORY] = jnp.zeros((HISTORY,) + out.shape[1:], out.dtype)


def ring_turn(volts):
    inputs = volts.shape[0]
    per = inputs // RING
    chunks = per // CHUNK
    return pl.pallas_call(
        functools.partial(ring_turn_kernel, per),
        out_shape=jax.ShapeDtypeStruct((RING + HISTORY, per) + volts.shape[1:], volts.dtype),
        in_specs=[pl.BlockSpec(memory_space=pl.ANY)],
        out_specs=pl.BlockSpec(memory_space=pltpu.VMEM),
        scratch_shapes=[
            pltpu.SemaphoreType.DMA,
            pltpu.SemaphoreType.DMA((chunks, 2)),
            pltpu.SemaphoreType.DMA,
            pltpu.SemaphoreType.DMA((chunks,)),
        ],
        compiler_params=pltpu.CompilerParams(collective_id=0, has_side_effects=True),
    )(volts)


def spectra_chunk(k, frames, coeffs, first, second, order, cosine, sine, stage, out):
    half = CHANNELS
    taps = [jnp.concatenate([coeffs[t], coeffs[t]], 0) for t in range(TAPS)]

    def pair(step, carry):
        sections = []
        for j in range(2):
            source = k * CHUNK + step * 2 + j
            held = [frames[t, source].astype(jnp.float32) for t in range(RING + HISTORY)]
            rows = []
            for t in range(RING):
                total = taps[0] * held[t + HISTORY]
                for tap in range(1, TAPS):
                    total = total + taps[tap] * held[t + HISTORY - tap]
                rows.append(total.astype(jnp.bfloat16))
            sections.append(jnp.concatenate(rows, 0))
        filtered = jnp.concatenate(sections, 1)
        one = jnp.dot(first[...], filtered, preferred_element_type=jnp.float32)
        cos_tw = cosine[...]
        sin_tw = sine[...]
        twisted = []
        for j in range(2):
            lanes = slice(j * LANES, (j + 1) * LANES)
            real = one[:half, lanes]
            imag = one[half:, lanes]
            tw_real = real * cos_tw + imag * sin_tw
            tw_imag = imag * cos_tw - real * sin_tw
            twisted.append(jnp.concatenate([tw_real, tw_imag], 1).astype(jnp.bfloat16))
        spectra = lax.dot_general(
            second[...],
            jnp.concatenate(twisted, 0),
            (((1,), (1,)), ((), ())),
            preferred_element_type=jnp.float32,
        ).astype(jnp.bfloat16)
        for j in range(2):
            rows = pl.ds(pl.multiple_of((step * 2 + j) * CHUNK, CHUNK), CHUNK)
            for part in range(2):
                for group in range(CHANNELS // CHUNK):
                    start = part * CHANNELS + group * CHUNK
                    stage[group, rows, part * LANES : (part + 1) * LANES] = spectra[
                        start : start + CHUNK, j * LANES : (j + 1) * LANES
                    ]
        return carry

    lax.fori_loop(0, CHUNK // 2, pair, 0)

    def turn(group, carry):
        turned = jnp.dot(order[...], stage[group], preferred_element_type=jnp.float32)
        turned = turned.astype(jnp.bfloat16).reshape(CHUNK, CHUNK, 2 * LANES)
        out[k, pl.ds(group * CHUNK, CHUNK)] = turned
        return carry

    lax.fori_loop(0, CHANNELS // CHUNK, turn, 0)


def spectra_kernel(frames, coeffs, first, second, order, cosine, sine, out, stage):
    for k in range(out.shape[0]):
        spectra_chunk(k, frames, coeffs, first, second, order, cosine, sine, stage, out)


def make_spectra(frames, coeffs, constants):
    per = frames.shape[1]
    vmem = pl.BlockSpec(memory_space=pltpu.VMEM)
    return pl.pallas_call(
        spectra_kernel,
        out_shape=jax.ShapeDtypeStruct(
            (per // CHUNK, CHANNELS, CHUNK, 2 * LANES), jnp.bfloat16
        ),
        in_specs=[vmem] * 7,
        out_specs=vmem,
        scratch_shapes=[pltpu.VMEM((CHANNELS // CHUNK, CHUNK * CHUNK, 2 * LANES), jnp.bfloat16)],
    )(frames, coeffs, *constants)


def correlate(rows, columns, total):
    depth = rows.shape[-1]
    pieces = []
    for start in range(0, depth, 2 * LANES):
        pieces.append(rows[:, start + LANES : start + 2 * LANES])
        pieces.append(-rows[:, start : start + LANES])
    flipped = jnp.concatenate(pieces, 1)
    contract = (((1,), (1,)), ((), ()))
    total[0] += lax.dot_general(rows, columns, contract, preferred_element_type=jnp.float32)
    total[1] += lax.dot_general(flipped, columns, contract, preferred_element_type=jnp.float32)


def corner_kernel(
    spectra,
    autos,
    cross,
    held,
    partial,
    incoming,
    send_sem,
    recv_sem,
    cross_sem,
    forward_sem,
    sum_sem,
    own_sem,
):
    me = lax.axis_index("inner")
    group = lax.axis_index("group")
    other = 1 - group
    ring = lax.rem(me, RING)
    zee = lax.rem(me // RING, ZS)
    ex = me // (RING * ZS)
    towards = 2 * group - 1
    plane = RING * XS
    parts = spectra.shape[0]
    inputs = parts * CHUNK * RING

    def place(step, zed):
        x_to = lax.rem(ex + step // RING, XS)
        ring_to = lax.rem(ring + lax.rem(step, RING), RING)
        return (x_to * ZS + zed) * RING + ring_to

    def at_distance(distance):
        return lax.rem(zee + distance + 2 * ZS, ZS)

    barrier = pltpu.get_barrier_semaphore()

    def greet(group_to, zed, begin):
        def body(step, carry):
            pl.semaphore_signal(
                barrier,
                inc=1,
                device_id={"group": group_to, "inner": place(step, zed)},
                device_id_type=MESH_ID,
            )
            return carry

        lax.fori_loop(begin, plane, body, 0)

    for distance in range(ZS):
        greet(group, at_distance(distance), 1 if distance == 0 else 0)
    greet(other, zee, 0)
    greet(other, at_distance(towards), 0)
    lanes_here = pl.ds(pl.multiple_of(ex * 2 * LANES, 2 * LANES), 2 * LANES)
    rows_here = pl.ds(ring * parts, parts)

    own = pltpu.make_async_copy(
        spectra.at[:, me], held.at[group, 0, rows_here, :, lanes_here], own_sem
    )
    own.start()
    autos[...] = jnp.zeros(autos.shape, autos.dtype)
    partial[...] = jnp.zeros(partial.shape, partial.dtype)
    pl.semaphore_wait(barrier, (ZS + 2) * plane - 1)

    def send(group_to, zed, begin, sem):
        slot = lax.rem(zee - zed + ZS, ZS)

        def body(step, carry):
            peer = place(step, zed)
            pltpu.make_async_remote_copy(
                src_ref=spectra.at[:, peer],
                dst_ref=held.at[group, slot, rows_here, :, lanes_here],
                send_sem=send_sem,
                recv_sem=sem.at[slot],
                device_id={"group": group_to, "inner": peer},
                device_id_type=MESH_ID,
            ).start()
            return carry

        lax.fori_loop(begin, plane, body, 0)

    send(group, at_distance(2), 0, recv_sem)
    send(group, zee, 1, recv_sem)

    @pl.when(ex // 2 == group)
    def _():
        send(other, zee, 0, cross_sem)

    send(group, at_distance(-towards), 0, recv_sem)
    send(other, at_distance(towards), 0, cross_sem)
    send(group, at_distance(towards), 0, recv_sem)

    near = lax.rem(towards + ZS, ZS)
    own_half = pl.ds(pl.multiple_of(group * 4 * LANES, 4 * LANES), 4 * LANES)
    other_half = pl.ds(pl.multiple_of(other * 4 * LANES, 4 * LANES), 4 * LANES)

    def arrived(ref, sem):
        pltpu.make_async_copy(ref, ref, sem).wait()

    def flat(slot, which, lanes=slice(None)):
        block = held[which, slot, :, :, lanes]
        return block.reshape(inputs, block.shape[-1])

    own.wait()
    arrived(spectra.at[:, pl.ds(0, plane - 1)], recv_sem.at[0])
    mine = flat(0, group)
    correlate(mine, mine, autos)
    arrived(held.at[other, 0, :, :, other_half], cross_sem.at[0])
    correlate(flat(0, 1, other_half), flat(0, 0, other_half), partial)
    arrived(held.at[group, 2], recv_sem.at[2])
    forward = pltpu.make_async_remote_copy(
        src_ref=held.at[group, 2, :, :, own_half],
        dst_ref=held.at[group, 2, :, :, own_half],
        send_sem=forward_sem.at[0],
        recv_sem=forward_sem.at[1],
        device_id={"group": other},
        device_id_type=MESH_ID,
    )
    forward.start()
    mine = flat(2, group)
    correlate(mine, mine, autos)
    arrived(held.at[group, near], recv_sem.at[near])
    mine = flat(near, group)
    correlate(mine, mine, autos)
    arrived(held.at[other, near], cross_sem.at[near])
    correlate(flat(near, 1), flat(near, 0), partial)
    arrived(held.at[other, 2, :, :, other_half], forward_sem.at[1])
    correlate(flat(2, 1, other_half), flat(2, 0, other_half), partial)
    keep = inputs // 2
    swap = pltpu.make_async_remote_copy(
        src_ref=partial.at[:, pl.ds(pl.multiple_of(other * keep, keep), keep)],
        dst_ref=incoming,
        send_sem=sum_sem.at[0],
        recv_sem=sum_sem.at[1],
        device_id={"group": other},
        device_id_type=MESH_ID,
    )
    swap.start()
    far = lax.rem(ZS - towards, ZS)
    arrived(held.at[group, far], recv_sem.at[far])
    mine = flat(far, group)
    correlate(mine, mine, autos)
    scale = 1.0 / (RING * BLOCKS * SUBCHANNELS)
    autos[...] = autos[...] * scale
    swap.wait()
    kept = partial[:, pl.ds(pl.multiple_of(group * keep, keep), keep)]
    cross[...] = (kept + incoming[...]) * scale
    arrived(spectra.at[:, pl.ds(0, ZS * plane - 1)], send_sem)
    arrived(spectra.at[:, pl.ds(0, plane)], send_sem)

    @pl.when(ex // 2 == group)
    def _():
        arrived(spectra.at[:, pl.ds(0, plane)], send_sem)

    forward.wait_send()


def corner(spectra):
    parts = spectra.shape[0]
    inputs = parts * CHUNK * RING
    vmem = pl.BlockSpec(memory_space=pltpu.VMEM)
    return pl.pallas_call(
        corner_kernel,
        out_shape=(
            jax.ShapeDtypeStruct((2, inputs, inputs), jnp.float32),
            jax.ShapeDtypeStruct((2, inputs // 2, inputs), jnp.float32),
        ),
        in_specs=[vmem],
        out_specs=(vmem, vmem),
        scratch_shapes=[
            pltpu.VMEM((2, ZS, parts * RING, CHUNK, XS * 2 * LANES), jnp.bfloat16),
            pltpu.VMEM((2, inputs, inputs), jnp.float32),
            pltpu.VMEM((2, inputs // 2, inputs), jnp.float32),
            pltpu.SemaphoreType.DMA,
            pltpu.SemaphoreType.DMA((ZS,)),
            pltpu.SemaphoreType.DMA((ZS,)),
            pltpu.SemaphoreType.DMA((2,)),
            pltpu.SemaphoreType.DMA((2,)),
            pltpu.SemaphoreType.DMA,
        ],
        compiler_params=pltpu.CompilerParams(collective_id=1, has_side_effects=True),
    )(spectra)


def shards(voltages, coeffs):
    volts = voltages.reshape(voltages.shape[1], 2 * SUBCHANNELS, CHANNELS)
    frames = ring_turn(volts)
    spectra = make_spectra(frames, coeffs, tables())
    autos, cross = corner(spectra)
    return (autos[None], cross[None])


def solution(mesh):
    placed = (P("inner", "group", None, None, None), P())
    return jax.shard_map(
        shards,
        mesh=mesh,
        in_specs=placed,
        out_specs=(P("inner", None, "group", None), P("inner", None, "group", None)),
        check_vma=False,
    )
```

```python
import functools
import math

import jax
import jax.numpy as jnp
import numpy as np
from jax import lax
from jax.experimental import pallas as pl
from jax.experimental.pallas import tpu as pltpu
from jax.sharding import PartitionSpec as P

MESH_ID = pl.DeviceIdType.MESH
SUBCHANNELS = 16
TAPS = 3
CHANNELS = 128
RING = 8
BLOCKS = 16
ZS = 4
XS = 4
HISTORY = TAPS - 1
LANES = 128
CHUNK = 16


def dft_block(length_dft):
    indices = np.arange(length_dft)
    angles = 2.0 * np.pi * (indices[:, None] * indices[None, :] % length_dft) / length_dft
    cosine = np.cos(angles)
    sine_table = np.sin(angles)
    upper = np.stack([cosine, -sine_table], axis=1)
    lower = np.stack([sine_table, cosine], axis=1)
    return np.stack([upper, lower], axis=0)


def twiddle_tables(channel_count):
    fine_count = SUBCHANNELS * channel_count
    rows_k = np.arange(SUBCHANNELS)[:, None]
    cols_q = np.arange(channel_count)[None, :]
    angles = 2.0 * np.pi * (rows_k * cols_q % fine_count) / fine_count
    factor = 1.0 / math.sqrt(fine_count)
    return (np.cos(angles) * factor, np.sin(angles) * factor)


def tables():
    small = dft_block(SUBCHANNELS)
    first = np.einsum("fg,rpsk->sfkgrp", np.eye(RING), small)
    rows = RING * 2 * SUBCHANNELS
    first = first.reshape(rows, rows)
    second = dft_block(CHANNELS).reshape(2 * CHANNELS, 2 * CHANNELS).T
    order = np.einsum("ij,mn->mijn", np.eye(CHUNK), np.eye(CHUNK))
    order = order.reshape(CHUNK * CHUNK, CHUNK * CHUNK)
    cos_np, sin_np = twiddle_tables(CHANNELS)
    as_bf16 = [jnp.asarray(t, jnp.float32).astype(jnp.bfloat16) for t in (first, second, order)]
    as_f32 = [jnp.asarray(np.tile(t, (RING, 1)), jnp.float32) for t in (cos_np, sin_np)]
    return as_bf16 + as_f32


def spectra_chunk(k, frames, coeffs, first, second, order, cosine, sine, stage, out):
    half = CHANNELS
    taps = [jnp.concatenate([coeffs[t], coeffs[t]], 0) for t in range(TAPS)]

    def pair(step, carry):
        sections = []
        for j in range(2):
            source = k * CHUNK + step * 2 + j
            held = [frames[t, source].astype(jnp.float32) for t in range(RING + HISTORY)]
            rows = []
            for t in range(RING):
                total = taps[0] * held[t + HISTORY]
                for tap in range(1, TAPS):
                    total = total + taps[tap] * held[t + HISTORY - tap]
                rows.append(total.astype(jnp.bfloat16))
            sections.append(jnp.concatenate(rows, 0))
        filtered = jnp.concatenate(sections, 1)
        one = jnp.dot(first[...], filtered, preferred_element_type=jnp.float32)
        cos_tw = cosine[...]
        sin_tw = sine[...]
        twisted = []
        for j in range(2):
            lanes = slice(j * LANES, (j + 1) * LANES)
            real = one[:half, lanes]
            imag = one[half:, lanes]
            tw_real = real * cos_tw + imag * sin_tw
            tw_imag = imag * cos_tw - real * sin_tw
            twisted.append(jnp.concatenate([tw_real, tw_imag], 1).astype(jnp.bfloat16))
        spectra = lax.dot_general(
            second[...],
            jnp.concatenate(twisted, 0),
            (((1,), (1,)), ((), ())),
            preferred_element_type=jnp.float32,
        ).astype(jnp.bfloat16)
        for j in range(2):
            rows = pl.ds(pl.multiple_of((step * 2 + j) * CHUNK, CHUNK), CHUNK)
            for part in range(2):
                for group in range(CHANNELS // CHUNK):
                    start = part * CHANNELS + group * CHUNK
                    stage[group, rows, part * LANES : (part + 1) * LANES] = spectra[
                        start : start + CHUNK, j * LANES : (j + 1) * LANES
                    ]
        return carry

    lax.fori_loop(0, CHUNK // 2, pair, 0)

    def turn(group, carry):
        turned = jnp.dot(order[...], stage[group], preferred_element_type=jnp.float32)
        turned = turned.astype(jnp.bfloat16).reshape(CHUNK, CHUNK, 2 * LANES)
        out[k, pl.ds(group * CHUNK, CHUNK)] = turned
        return carry

    lax.fori_loop(0, CHANNELS // CHUNK, turn, 0)


def correlate(rows, columns, total, row_start, column_start):
    pieces = []
    for start in range(0, rows.shape[1], 2 * LANES):
        pieces.append(rows[:, start + LANES : start + 2 * LANES])
        pieces.append(-rows[:, start : start + LANES])
    flipped = jnp.concatenate(pieces, 1)
    contract = (((1,), (1,)), ((), ()))
    row_range = slice(row_start, row_start + rows.shape[0])
    column_range = slice(column_start, column_start + columns.shape[0])
    for part, left in enumerate((rows, flipped)):
        total[part, row_range, column_range] += lax.dot_general(
            left, columns, contract, preferred_element_type=jnp.float32
        )


def whole_kernel(
    volts,
    coeffs,
    first,
    second,
    order,
    cosine,
    sine,
    autos,
    cross,
    frames,
    stage,
    spectra,
    held,
    partial,
    incoming,
    turn_send,
    turn_recv,
    halo_send,
    halo_recv,
    send_sem,
    recv_sem,
    cross_sem,
    pass_send,
    pass_recv,
    sum_sem,
):
    me = lax.axis_index("inner")
    group = lax.axis_index("group")
    count = lax.axis_size("inner")
    other = 1 - group
    ring = lax.rem(me, RING)
    base = me - ring
    following = lax.rem(me + RING, count)
    tail = ring // (RING - HISTORY)
    zee = lax.rem(me // RING, ZS)
    ex = me // (RING * ZS)
    towards = 2 * group - 1
    plane = RING * XS
    chunks = spectra.shape[0]
    near = lax.rem(towards + ZS, ZS)
    far = lax.rem(ZS - towards, ZS)
    my_half = ex // (XS // 2)
    crossing = lax.rem(my_half + group, 2)
    staying = 1 - crossing
    met = lax.rem(my_half + other, 2)

    def at_distance(distance):
        return lax.rem(zee + distance + 2 * ZS, ZS)

    def place(step, zed):
        x_to = lax.rem(ex + step // RING, XS)
        ring_to = lax.rem(ring + lax.rem(step, RING), RING)
        return (x_to * ZS + zed) * RING + ring_to

    def to_half(half):
        def locate(step, zed):
            x_to = half * (XS // 2) + step // RING
            ring_to = lax.rem(ring + lax.rem(step, RING), RING)
            return (x_to * ZS + zed) * RING + ring_to

        return locate

    def x_lanes(x, width=1):
        return pl.ds(pl.multiple_of(x * 2 * LANES, 2 * LANES), width * 2 * LANES)

    def half_lanes(half):
        return x_lanes(half * (XS // 2), XS // 2)

    def arrived(ref, sem):
        pltpu.make_async_copy(ref, ref, sem).wait()

    barrier = pltpu.get_barrier_semaphore()

    def greet(group_to, zed, begin):
        def body(step, carry):
            pl.semaphore_signal(
                barrier,
                inc=1,
                device_id={"group": group_to, "inner": place(step, zed)},
                device_id_type=MESH_ID,
            )
            return carry

        lax.fori_loop(begin, plane, body, 0)

    for distance in range(ZS):
        greet(group, at_distance(distance), 1 if distance == 0 else 0)
    greet(other, zee, 0)
    greet(other, at_distance(towards), 0)
    greet(other, at_distance(2), 0)
    pl.semaphore_wait(barrier, (ZS + 3) * plane - 1)

    for k in range(chunks):
        mine = pl.ds(k * CHUNK, CHUNK)
        for s in range(1, RING):
            owner = lax.rem(ring + s, RING)
            pltpu.make_async_remote_copy(
                src_ref=volts.at[pl.ds((k * RING + owner) * CHUNK, CHUNK)],
                dst_ref=frames.at[HISTORY + ring, mine],
                send_sem=turn_send,
                recv_sem=turn_recv.at[k, tail],
                device_id={"inner": base + owner},
                device_id_type=MESH_ID,
            ).start()
        pltpu.make_async_copy(
            volts.at[pl.ds((k * RING + ring) * CHUNK, CHUNK)],
            frames.at[HISTORY + ring, mine],
            turn_recv.at[k, tail],
        ).start()

    def send_halo(k):
        mine = pl.ds(k * CHUNK, CHUNK)
        last = frames.at[pl.ds(RING, HISTORY), mine]
        arrived(last, turn_recv.at[k, 1])
        pltpu.make_async_remote_copy(
            src_ref=last,
            dst_ref=frames.at[pl.ds(0, HISTORY), mine],
            send_sem=halo_send,
            recv_sem=halo_recv.at[k],
            device_id={"inner": following},
            device_id_type=MESH_ID,
        ).start()

    def channelize(k):
        mine = pl.ds(k * CHUNK, CHUNK)
        arrived(frames.at[pl.ds(HISTORY, RING - HISTORY), mine], turn_recv.at[k, 0])
        arrived(frames.at[pl.ds(0, HISTORY), mine], halo_recv.at[k])

        @pl.when(me < RING)
        def _():
            frames[0:HISTORY, mine] = jnp.zeros(
                (HISTORY, CHUNK) + frames.shape[2:], frames.dtype
            )

        spectra_chunk(k, frames, coeffs, first, second, order, cosine, sine, stage, spectra)

    def send_spectra(k):
        row = k * RING + ring

        def send(group_to, zed, locate, begin, end, sem):
            slot = lax.rem(zee - zed + ZS, ZS)

            def body(step, carry):
                peer = locate(step, zed)
                pltpu.make_async_remote_copy(
                    src_ref=spectra.at[k, peer],
                    dst_ref=held.at[group, slot, row, :, x_lanes(ex)],
                    send_sem=send_sem,
                    recv_sem=sem(slot),
                    device_id={"group": group_to, "inner": peer},
                    device_id_type=MESH_ID,
                ).start()
                return carry

            lax.fori_loop(begin, end, body, 0)

        def by_slot(slot):
            return recv_sem.at[slot, k]

        def by_source(slot):
            return cross_sem.at[slot, k, ex]

        send(other, at_distance(towards), place, 0, plane, by_source)
        send(other, at_distance(2), to_half(crossing), 0, plane // 2, by_source)
        send(group, at_distance(2), to_half(staying), 0, plane // 2, by_slot)
        send(group, at_distance(-towards), place, 0, plane, by_slot)
        send(other, zee, to_half(crossing), 0, plane // 2, by_source)
        send(group, zee, place, 1, plane, by_slot)
        pltpu.make_async_copy(
            spectra.at[k, me], held.at[group, 0, row, :, x_lanes(ex)], recv_sem.at[0, k]
        ).start()

    def chunk_rows(k):
        return pl.ds(k * RING, RING)

    def hand_on(k):
        for x in range(XS):
            here = lax.rem(ex + XS - x, XS)
            pass_on(k, near, here, recv_sem.at[near, k])
        for x in range(XS // 2):
            pass_on(k, 2, met * (XS // 2) + x, pass_recv.at[k])

    def pass_on(k, slot, x, sem):
        block = held.at[other, slot, chunk_rows(k), :, x_lanes(x)]
        arrived(block, cross_sem.at[slot, k, x])
        pltpu.make_async_remote_copy(
            src_ref=block,
            dst_ref=block,
            send_sem=pass_send,
            recv_sem=sem,
            device_id={"group": other},
            device_id_type=MESH_ID,
        ).start()

    def flat(which, slot, begin, end, lanes=slice(None)):
        block = held[which, slot, begin * RING : end * RING, :, lanes]
        return block.reshape((end - begin) * RING * CHUNK, block.shape[-1])

    size = RING * CHUNK

    def add_early(which_rows, which_columns, slot, total, lanes=slice(None)):
        last = chunks - 1
        rows = flat(which_rows, slot, 0, last, lanes)
        columns = flat(which_columns, slot, 0, last, lanes)
        correlate(rows, columns, total, 0, 0)

    def add_late(which_rows, which_columns, slot, total, lanes=slice(None)):
        last = chunks - 1
        columns = flat(which_columns, slot, 0, chunks, lanes)
        correlate(flat(which_rows, slot, last, chunks, lanes), columns, total, last * size, 0)
        correlate(
            flat(which_rows, slot, 0, last, lanes), columns[last * size :], total, 0, last * size
        )

    def wait_own(slot, k):
        arrived(held.at[group, slot, chunk_rows(k)], recv_sem.at[slot, k])

    def wait_staying(k):
        arrived(held.at[group, 2, chunk_rows(k), :, half_lanes(met)], recv_sem.at[2, k])

    def wait_passed(k):
        arrived(held.at[group, 2, chunk_rows(k), :, half_lanes(1 - met)], pass_recv.at[k])

    def wait_level(k):
        for x in range(XS // 2):
            here = met * (XS // 2) + x
            arrived(
                held.at[other, 0, chunk_rows(k), :, x_lanes(here)], cross_sem.at[0, k, here]
            )

    send_halo(0)
    send_halo(1)
    channelize(0)
    send_spectra(0)
    send_halo(2)
    channelize(1)
    send_spectra(1)
    hand_on(0)
    autos[...] = jnp.zeros(autos.shape, autos.dtype)
    partial[...] = jnp.zeros(partial.shape, partial.dtype)
    channelize(2)
    send_spectra(2)
    hand_on(1)
    for k in range(2):
        wait_own(0, k)
        wait_level(k)
    add_early(group, group, 0, autos)
    add_early(1, 0, 0, partial, half_lanes(met))
    hand_on(2)
    for k in range(2):
        wait_own(near, k)
    add_early(1, 0, near, partial)
    add_early(group, group, near, autos)
    for k in range(2):
        wait_staying(k)
    add_early(1, 0, 2, partial, half_lanes(met))
    for k in range(2):
        wait_passed(k)
    add_early(group, group, 2, autos)
    for k in range(2):
        wait_own(far, k)
    add_early(group, group, far, autos)
    wait_own(0, 2)
    wait_level(2)
    add_late(1, 0, 0, partial, half_lanes(met))
    wait_own(near, 2)
    add_late(1, 0, near, partial)
    wait_staying(2)
    add_late(1, 0, 2, partial, half_lanes(met))
    keep = chunks * size // 2
    swap = pltpu.make_async_remote_copy(
        src_ref=partial.at[:, pl.ds(pl.multiple_of(other * keep, keep), keep)],
        dst_ref=incoming,
        send_sem=sum_sem.at[0],
        recv_sem=sum_sem.at[1],
        device_id={"group": other},
        device_id_type=MESH_ID,
    )
    swap.start()
    add_late(group, group, 0, autos)
    add_late(group, group, near, autos)
    wait_passed(2)
    add_late(group, group, 2, autos)
    wait_own(far, 2)
    add_late(group, group, far, autos)
    swap.wait()
    cross[...] = partial[:, pl.ds(pl.multiple_of(group * keep, keep), keep)] + incoming[...]
    arrived(volts.at[pl.ds(0, (RING - 1) * chunks * CHUNK)], turn_send)
    arrived(frames.at[pl.ds(0, HISTORY)], halo_send)
    arrived(spectra.at[:, pl.ds(0, ZS * plane - 1)], send_sem)
    arrived(spectra.at[:, pl.ds(0, plane // 2)], send_sem)
    arrived(held.at[other, near], pass_send)
    arrived(held.at[other, 2, :, :, half_lanes(met)], pass_send)


def shards(voltages, coeffs):
    inputs = voltages.shape[1]
    volts = voltages.reshape(inputs, 2 * SUBCHANNELS, CHANNELS)
    chunks = inputs // (RING * CHUNK)
    vmem = pl.BlockSpec(memory_space=pltpu.VMEM)
    autos, cross = pl.pallas_call(
        whole_kernel,
        out_shape=(
            jax.ShapeDtypeStruct((2, inputs, inputs), jnp.float32),
            jax.ShapeDtypeStruct((2, inputs // 2, inputs), jnp.float32),
        ),
        in_specs=[pl.BlockSpec(memory_space=pl.ANY)] + [vmem] * 6,
        out_specs=(vmem, vmem),
        scratch_shapes=[
            pltpu.VMEM((RING + HISTORY, chunks * CHUNK) + volts.shape[1:], jnp.bfloat16),
            pltpu.VMEM((CHANNELS // CHUNK, CHUNK * CHUNK, 2 * LANES), jnp.bfloat16),
            pltpu.VMEM((chunks, CHANNELS, CHUNK, 2 * LANES), jnp.bfloat16),
            pltpu.VMEM((2, ZS, chunks * RING, CHUNK, XS * 2 * LANES), jnp.bfloat16),
            pltpu.VMEM((2, inputs, inputs), jnp.float32),
            pltpu.VMEM((2, inputs // 2, inputs), jnp.float32),
            pltpu.SemaphoreType.DMA,
            pltpu.SemaphoreType.DMA((chunks, 2)),
            pltpu.SemaphoreType.DMA,
            pltpu.SemaphoreType.DMA((chunks,)),
            pltpu.SemaphoreType.DMA,
            pltpu.SemaphoreType.DMA((ZS, chunks)),
            pltpu.SemaphoreType.DMA((ZS, chunks, XS)),
            pltpu.SemaphoreType.DMA,
            pltpu.SemaphoreType.DMA((chunks,)),
            pltpu.SemaphoreType.DMA((2,)),
        ],
        compiler_params=pltpu.CompilerParams(collective_id=0, has_side_effects=True),
    )(volts, coeffs, *tables())
    scale = 1.0 / (RING * BLOCKS * SUBCHANNELS)
    return (autos[None] * scale, cross[None] * scale)


def solution(mesh):
    placed = (P("inner", "group", None, None, None), P())
    return jax.shard_map(
        shards,
        mesh=mesh,
        in_specs=placed,
        out_specs=(P("inner", None, "group", None), P("inner", None, "group", None)),
        check_vma=False,
    )
```

```python
import functools
import math

import jax
import jax.numpy as jnp
import numpy as np
from jax import lax
from jax.experimental import pallas as pl
from jax.experimental.pallas import tpu as pltpu
from jax.sharding import PartitionSpec as P

MESH_ID = pl.DeviceIdType.MESH
SUBCHANNELS = 16
TAPS = 3
CHANNELS = 128
RING = 8
BLOCKS = 16
ZS = 4
XS = 4
HISTORY = TAPS - 1
LANES = 128
CHUNK = 16


def dft_block(length_dft):
    indices = np.arange(length_dft)
    angles = 2.0 * np.pi * (indices[:, None] * indices[None, :] % length_dft) / length_dft
    cosine = np.cos(angles)
    sine_table = np.sin(angles)
    upper = np.stack([cosine, -sine_table], axis=1)
    lower = np.stack([sine_table, cosine], axis=1)
    return np.stack([upper, lower], axis=0)


def twiddle_tables(channel_count):
    fine_count = SUBCHANNELS * channel_count
    rows_k = np.arange(SUBCHANNELS)[:, None]
    cols_q = np.arange(channel_count)[None, :]
    angles = 2.0 * np.pi * (rows_k * cols_q % fine_count) / fine_count
    factor = 1.0 / math.sqrt(fine_count)
    return (np.cos(angles) * factor, np.sin(angles) * factor)


def tables():
    small = dft_block(SUBCHANNELS)
    first = np.einsum("fg,rpsk->sfkgrp", np.eye(RING), small)
    rows = RING * 2 * SUBCHANNELS
    first = first.reshape(rows, rows)
    second = dft_block(CHANNELS).reshape(2 * CHANNELS, 2 * CHANNELS).T
    order = np.einsum("ij,mn->mijn", np.eye(CHUNK), np.eye(CHUNK))
    order = order.reshape(CHUNK * CHUNK, CHUNK * CHUNK)
    cos_np, sin_np = twiddle_tables(CHANNELS)
    as_bf16 = [jnp.asarray(t, jnp.float32).astype(jnp.bfloat16) for t in (first, second, order)]
    as_f32 = [jnp.asarray(np.tile(t, (RING, 1)), jnp.float32) for t in (cos_np, sin_np)]
    return as_bf16 + as_f32


def spectra_chunk(k, frames, coeffs, first, second, order, cosine, sine, stage, out):
    half = CHANNELS
    taps = [jnp.concatenate([coeffs[t], coeffs[t]], 0) for t in range(TAPS)]

    def pair(step, carry):
        sections = []
        for j in range(2):
            source = k * CHUNK + step * 2 + j
            held = [frames[t, source].astype(jnp.float32) for t in range(RING + HISTORY)]
            rows = []
            for t in range(RING):
                total = taps[0] * held[t + HISTORY]
                for tap in range(1, TAPS):
                    total = total + taps[tap] * held[t + HISTORY - tap]
                rows.append(total.astype(jnp.bfloat16))
            sections.append(jnp.concatenate(rows, 0))
        filtered = jnp.concatenate(sections, 1)
        one = jnp.dot(first[...], filtered, preferred_element_type=jnp.float32)
        cos_tw = cosine[...]
        sin_tw = sine[...]
        twisted = []
        for j in range(2):
            lanes = slice(j * LANES, (j + 1) * LANES)
            real = one[:half, lanes]
            imag = one[half:, lanes]
            tw_real = real * cos_tw + imag * sin_tw
            tw_imag = imag * cos_tw - real * sin_tw
            twisted.append(jnp.concatenate([tw_real, tw_imag], 1).astype(jnp.bfloat16))
        spectra = lax.dot_general(
            second[...],
            jnp.concatenate(twisted, 0),
            (((1,), (1,)), ((), ())),
            preferred_element_type=jnp.float32,
        ).astype(jnp.bfloat16)
        for j in range(2):
            rows = pl.ds(pl.multiple_of((step * 2 + j) * CHUNK, CHUNK), CHUNK)
            for part in range(2):
                for group in range(CHANNELS // CHUNK):
                    start = part * CHANNELS + group * CHUNK
                    stage[group, rows, part * LANES : (part + 1) * LANES] = spectra[
                        start : start + CHUNK, j * LANES : (j + 1) * LANES
                    ]
        return carry

    lax.fori_loop(0, CHUNK // 2, pair, 0)

    def turn(group, carry):
        turned = jnp.dot(order[...], stage[group], preferred_element_type=jnp.float32)
        turned = turned.astype(jnp.bfloat16).reshape(CHUNK, CHUNK, 2 * LANES)
        out[k, pl.ds(group * CHUNK, CHUNK)] = turned
        return carry

    lax.fori_loop(0, CHANNELS // CHUNK, turn, 0)


def correlate(rows, columns, total, row_start, column_start):
    pieces = []
    for start in range(0, rows.shape[1], 2 * LANES):
        pieces.append(rows[:, start + LANES : start + 2 * LANES])
        pieces.append(-rows[:, start : start + LANES])
    flipped = jnp.concatenate(pieces, 1)
    contract = (((1,), (1,)), ((), ()))
    row_range = slice(row_start, row_start + rows.shape[0])
    column_range = slice(column_start, column_start + columns.shape[0])
    for part, left in enumerate((rows, flipped)):
        total[part, row_range, column_range] += lax.dot_general(
            left, columns, contract, preferred_element_type=jnp.float32
        )


def whole_kernel(
    volts,
    coeffs,
    first,
    second,
    order,
    cosine,
    sine,
    autos,
    cross,
    frames,
    stage,
    spectra,
    held,
    partial,
    outgoing,
    incoming,
    turn_send,
    turn_recv,
    halo_send,
    halo_recv,
    send_sem,
    recv_sem,
    cross_sem,
    pass_send,
    pass_recv,
    sum_sem,
):
    me = lax.axis_index("inner")
    group = lax.axis_index("group")
    count = lax.axis_size("inner")
    other = 1 - group
    ring = lax.rem(me, RING)
    base = me - ring
    following = lax.rem(me + RING, count)
    tail = ring // (RING - HISTORY)
    zee = lax.rem(me // RING, ZS)
    ex = me // (RING * ZS)
    towards = 2 * group - 1
    plane = RING * XS
    chunks = spectra.shape[0]
    near = lax.rem(towards + ZS, ZS)
    far = lax.rem(ZS - towards, ZS)
    my_half = ex // (XS // 2)
    crossing = lax.rem(my_half + group, 2)
    staying = 1 - crossing
    met = lax.rem(my_half + other, 2)

    def at_distance(distance):
        return lax.rem(zee + distance + 2 * ZS, ZS)

    def place(step, zed):
        x_to = lax.rem(ex + step // RING, XS)
        ring_to = lax.rem(ring + lax.rem(step, RING), RING)
        return (x_to * ZS + zed) * RING + ring_to

    def to_half(half):
        def locate(step, zed):
            x_to = half * (XS // 2) + step // RING
            ring_to = lax.rem(ring + lax.rem(step, RING), RING)
            return (x_to * ZS + zed) * RING + ring_to

        return locate

    def x_lanes(x, width=1):
        return pl.ds(pl.multiple_of(x * 2 * LANES, 2 * LANES), width * 2 * LANES)

    def half_lanes(half):
        return x_lanes(half * (XS // 2), XS // 2)

    def arrived(ref, sem):
        pltpu.make_async_copy(ref, ref, sem).wait()

    barrier = pltpu.get_barrier_semaphore()

    def greet(group_to, zed, begin):
        def body(step, carry):
            pl.semaphore_signal(
                barrier,
                inc=1,
                device_id={"group": group_to, "inner": place(step, zed)},
                device_id_type=MESH_ID,
            )
            return carry

        lax.fori_loop(begin, plane, body, 0)

    for distance in range(ZS):
        greet(group, at_distance(distance), 1 if distance == 0 else 0)
    greet(other, zee, 0)
    greet(other, at_distance(towards), 0)
    greet(other, at_distance(2), 0)
    pl.semaphore_wait(barrier, (ZS + 3) * plane - 1)

    for k in range(chunks):
        mine = pl.ds(k * CHUNK, CHUNK)
        for s in range(1, RING):
            owner = lax.rem(ring + s, RING)
            pltpu.make_async_remote_copy(
                src_ref=volts.at[pl.ds((k * RING + owner) * CHUNK, CHUNK)],
                dst_ref=frames.at[HISTORY + ring, mine],
                send_sem=turn_send,
                recv_sem=turn_recv.at[k, tail],
                device_id={"inner": base + owner},
                device_id_type=MESH_ID,
            ).start()
        pltpu.make_async_copy(
            volts.at[pl.ds((k * RING + ring) * CHUNK, CHUNK)],
            frames.at[HISTORY + ring, mine],
            turn_recv.at[k, tail],
        ).start()

    def send_halo(k):
        mine = pl.ds(k * CHUNK, CHUNK)
        last = frames.at[pl.ds(RING, HISTORY), mine]
        arrived(last, turn_recv.at[k, 1])
        pltpu.make_async_remote_copy(
            src_ref=last,
            dst_ref=frames.at[pl.ds(0, HISTORY), mine],
            send_sem=halo_send,
            recv_sem=halo_recv.at[k],
            device_id={"inner": following},
            device_id_type=MESH_ID,
        ).start()

    def channelize(k):
        mine = pl.ds(k * CHUNK, CHUNK)
        arrived(frames.at[pl.ds(HISTORY, RING - HISTORY), mine], turn_recv.at[k, 0])
        arrived(frames.at[pl.ds(0, HISTORY), mine], halo_recv.at[k])

        @pl.when(me < RING)
        def _():
            frames[0:HISTORY, mine] = jnp.zeros(
                (HISTORY, CHUNK) + frames.shape[2:], frames.dtype
            )

        spectra_chunk(k, frames, coeffs, first, second, order, cosine, sine, stage, spectra)

    def send_spectra(k):
        row = k * RING + ring

        def send(group_to, zed, locate, begin, end, sem):
            slot = lax.rem(zee - zed + ZS, ZS)

            def body(step, carry):
                peer = locate(step, zed)
                pltpu.make_async_remote_copy(
                    src_ref=spectra.at[k, peer],
                    dst_ref=held.at[group, slot, row, :, x_lanes(ex)],
                    send_sem=send_sem,
                    recv_sem=sem(slot),
                    device_id={"group": group_to, "inner": peer},
                    device_id_type=MESH_ID,
                ).start()
                return carry

            lax.fori_loop(begin, end, body, 0)

        def by_slot(slot):
            return recv_sem.at[slot, k]

        def by_source(slot):
            return cross_sem.at[slot, k, ex]

        send(other, at_distance(towards), place, 0, plane, by_source)
        send(other, at_distance(2), to_half(crossing), 0, plane // 2, by_source)
        send(group, at_distance(2), to_half(staying), 0, plane // 2, by_slot)
        send(group, at_distance(-towards), place, 0, plane, by_slot)
        send(other, zee, to_half(crossing), 0, plane // 2, by_source)
        send(group, zee, place, 1, plane, by_slot)
        pltpu.make_async_copy(
            spectra.at[k, me], held.at[group, 0, row, :, x_lanes(ex)], recv_sem.at[0, k]
        ).start()

    def chunk_rows(k):
        return pl.ds(k * RING, RING)

    def hand_on(k):
        for x in range(XS):
            here = lax.rem(ex + XS - x, XS)
            pass_on(k, near, here, recv_sem.at[near, k])
        for x in range(XS // 2):
            pass_on(k, 2, met * (XS // 2) + x, pass_recv.at[k])

    def pass_on(k, slot, x, sem):
        block = held.at[other, slot, chunk_rows(k), :, x_lanes(x)]
        arrived(block, cross_sem.at[slot, k, x])
        pltpu.make_async_remote_copy(
            src_ref=block,
            dst_ref=block,
            send_sem=pass_send,
            recv_sem=sem,
            device_id={"group": other},
            device_id_type=MESH_ID,
        ).start()

    def flat(which, slot, begin, end, lanes=slice(None)):
        block = held[which, slot, begin * RING : end * RING, :, lanes]
        return block.reshape((end - begin) * RING * CHUNK, block.shape[-1])

    size = RING * CHUNK

    def add_early(which_rows, which_columns, slot, total, lanes=slice(None)):
        last = chunks - 1
        rows = flat(which_rows, slot, 0, last, lanes)
        columns = flat(which_columns, slot, 0, last, lanes)
        correlate(rows, columns, total, 0, 0)

    def add_late(which_rows, which_columns, slot, total, lanes=slice(None)):
        last = chunks - 1
        columns = flat(which_columns, slot, 0, chunks, lanes)
        correlate(flat(which_rows, slot, last, chunks, lanes), columns, total, last * size, 0)
        correlate(
            flat(which_rows, slot, 0, last, lanes), columns[last * size :], total, 0, last * size
        )

    def wait_own(slot, k):
        arrived(held.at[group, slot, chunk_rows(k)], recv_sem.at[slot, k])

    def wait_staying(k):
        arrived(held.at[group, 2, chunk_rows(k), :, half_lanes(met)], recv_sem.at[2, k])

    def wait_passed(k):
        arrived(held.at[group, 2, chunk_rows(k), :, half_lanes(1 - met)], pass_recv.at[k])

    def wait_level(k):
        for x in range(XS // 2):
            here = met * (XS // 2) + x
            arrived(
                held.at[other, 0, chunk_rows(k), :, x_lanes(here)], cross_sem.at[0, k, here]
            )

    send_halo(0)
    send_halo(1)
    channelize(0)
    send_spectra(0)
    send_halo(2)
    channelize(1)
    send_spectra(1)
    hand_on(0)
    autos[...] = jnp.zeros(autos.shape, autos.dtype)
    partial[...] = jnp.zeros(partial.shape, partial.dtype)
    channelize(2)
    send_spectra(2)
    hand_on(1)
    for k in range(2):
        wait_own(0, k)
        wait_level(k)
    add_early(group, group, 0, autos)
    add_early(1, 0, 0, partial, half_lanes(met))
    hand_on(2)
    for k in range(2):
        wait_own(near, k)
    add_early(1, 0, near, partial)
    add_early(group, group, near, autos)
    for k in range(2):
        wait_staying(k)
    add_early(1, 0, 2, partial, half_lanes(met))
    for k in range(2):
        wait_passed(k)
    add_early(group, group, 2, autos)
    for k in range(2):
        wait_own(far, k)
    add_early(group, group, far, autos)
    wait_own(0, 2)
    wait_level(2)
    add_late(1, 0, 0, partial, half_lanes(met))
    wait_own(near, 2)
    add_late(1, 0, near, partial)
    wait_staying(2)
    add_late(1, 0, 2, partial, half_lanes(met))
    keep = chunks * size // 2
    theirs = partial[:, pl.ds(pl.multiple_of(other * keep, keep), keep)]
    outgoing[...] = theirs.astype(outgoing.dtype)
    swap = pltpu.make_async_remote_copy(
        src_ref=outgoing,
        dst_ref=incoming,
        send_sem=sum_sem.at[0],
        recv_sem=sum_sem.at[1],
        device_id={"group": other},
        device_id_type=MESH_ID,
    )
    swap.start()
    add_late(group, group, 0, autos)
    add_late(group, group, near, autos)
    wait_passed(2)
    add_late(group, group, 2, autos)
    wait_own(far, 2)
    add_late(group, group, far, autos)
    swap.wait()
    kept = partial[:, pl.ds(pl.multiple_of(group * keep, keep), keep)]
    cross[...] = kept + incoming[...].astype(jnp.float32)
    arrived(volts.at[pl.ds(0, (RING - 1) * chunks * CHUNK)], turn_send)
    arrived(frames.at[pl.ds(0, HISTORY)], halo_send)
    arrived(spectra.at[:, pl.ds(0, ZS * plane - 1)], send_sem)
    arrived(spectra.at[:, pl.ds(0, plane // 2)], send_sem)
    arrived(held.at[other, near], pass_send)
    arrived(held.at[other, 2, :, :, half_lanes(met)], pass_send)


def shards(voltages, coeffs):
    inputs = voltages.shape[1]
    volts = voltages.reshape(inputs, 2 * SUBCHANNELS, CHANNELS)
    chunks = inputs // (RING * CHUNK)
    vmem = pl.BlockSpec(memory_space=pltpu.VMEM)
    autos, cross = pl.pallas_call(
        whole_kernel,
        out_shape=(
            jax.ShapeDtypeStruct((2, inputs, inputs), jnp.float32),
            jax.ShapeDtypeStruct((2, inputs // 2, inputs), jnp.float32),
        ),
        in_specs=[pl.BlockSpec(memory_space=pl.ANY)] + [vmem] * 6,
        out_specs=(vmem, vmem),
        scratch_shapes=[
            pltpu.VMEM((RING + HISTORY, chunks * CHUNK) + volts.shape[1:], jnp.bfloat16),
            pltpu.VMEM((CHANNELS // CHUNK, CHUNK * CHUNK, 2 * LANES), jnp.bfloat16),
            pltpu.VMEM((chunks, CHANNELS, CHUNK, 2 * LANES), jnp.bfloat16),
            pltpu.VMEM((2, ZS, chunks * RING, CHUNK, XS * 2 * LANES), jnp.bfloat16),
            pltpu.VMEM((2, inputs, inputs), jnp.float32),
            pltpu.VMEM((2, inputs // 2, inputs), jnp.bfloat16),
            pltpu.VMEM((2, inputs // 2, inputs), jnp.bfloat16),
            pltpu.SemaphoreType.DMA,
            pltpu.SemaphoreType.DMA((chunks, 2)),
            pltpu.SemaphoreType.DMA,
            pltpu.SemaphoreType.DMA((chunks,)),
            pltpu.SemaphoreType.DMA,
            pltpu.SemaphoreType.DMA((ZS, chunks)),
            pltpu.SemaphoreType.DMA((ZS, chunks, XS)),
            pltpu.SemaphoreType.DMA,
            pltpu.SemaphoreType.DMA((chunks,)),
            pltpu.SemaphoreType.DMA((2,)),
        ],
        compiler_params=pltpu.CompilerParams(collective_id=0, has_side_effects=True),
    )(volts, coeffs, *tables())
    scale = 1.0 / (RING * BLOCKS * SUBCHANNELS)
    return (autos[None] * scale, cross[None] * scale)


def solution(mesh):
    placed = (P("inner", "group", None, None, None), P())
    return jax.shard_map(
        shards,
        mesh=mesh,
        in_specs=placed,
        out_specs=(P("inner", None, "group", None), P("inner", None, "group", None)),
        check_vma=False,
    )
```

```python
import functools
import math

import jax
import jax.numpy as jnp
import numpy as np
from jax import lax
from jax.experimental import pallas as pl
from jax.experimental.pallas import tpu as pltpu
from jax.sharding import PartitionSpec as P

MESH_ID = pl.DeviceIdType.MESH
SUBCHANNELS = 16
TAPS = 3
CHANNELS = 128
RING = 8
BLOCKS = 16
ZS = 4
XS = 4
HISTORY = TAPS - 1
LANES = 128
CHUNK = 16


def dft_block(length_dft):
    indices = np.arange(length_dft)
    angles = 2.0 * np.pi * (indices[:, None] * indices[None, :] % length_dft) / length_dft
    cosine = np.cos(angles)
    sine_table = np.sin(angles)
    upper = np.stack([cosine, -sine_table], axis=1)
    lower = np.stack([sine_table, cosine], axis=1)
    return np.stack([upper, lower], axis=0)


def twiddle_tables(channel_count):
    fine_count = SUBCHANNELS * channel_count
    rows_k = np.arange(SUBCHANNELS)[:, None]
    cols_q = np.arange(channel_count)[None, :]
    angles = 2.0 * np.pi * (rows_k * cols_q % fine_count) / fine_count
    factor = 1.0 / math.sqrt(fine_count)
    return (np.cos(angles) * factor, np.sin(angles) * factor)


def tables():
    small = dft_block(SUBCHANNELS)
    first = np.einsum("fg,rpsk->sfkgrp", np.eye(RING), small)
    rows = RING * 2 * SUBCHANNELS
    first = first.reshape(rows, rows)
    second = dft_block(CHANNELS).reshape(2 * CHANNELS, 2 * CHANNELS).T
    order = np.einsum("ij,mn->mijn", np.eye(CHUNK), np.eye(CHUNK))
    order = order.reshape(CHUNK * CHUNK, CHUNK * CHUNK)
    cos_np, sin_np = twiddle_tables(CHANNELS)
    as_bf16 = [jnp.asarray(t, jnp.float32).astype(jnp.bfloat16) for t in (first, second, order)]
    as_f32 = [jnp.asarray(np.tile(t, (RING, 1)), jnp.float32) for t in (cos_np, sin_np)]
    return as_bf16 + as_f32


def spectra_chunk(k, frames, coeffs, first, second, order, cosine, sine, stage, out):
    half = CHANNELS
    taps = [jnp.concatenate([coeffs[t], coeffs[t]], 0) for t in range(TAPS)]

    def pair(step, carry):
        sections = []
        for j in range(2):
            source = k * CHUNK + step * 2 + j
            held = [frames[t, source].astype(jnp.float32) for t in range(RING + HISTORY)]
            rows = []
            for t in range(RING):
                total = taps[0] * held[t + HISTORY]
                for tap in range(1, TAPS):
                    total = total + taps[tap] * held[t + HISTORY - tap]
                rows.append(total.astype(jnp.bfloat16))
            sections.append(jnp.concatenate(rows, 0))
        filtered = jnp.concatenate(sections, 1)
        one = jnp.dot(first[...], filtered, preferred_element_type=jnp.float32)
        cos_tw = cosine[...]
        sin_tw = sine[...]
        twisted = []
        for j in range(2):
            lanes = slice(j * LANES, (j + 1) * LANES)
            real = one[:half, lanes]
            imag = one[half:, lanes]
            tw_real = real * cos_tw + imag * sin_tw
            tw_imag = imag * cos_tw - real * sin_tw
            twisted.append(jnp.concatenate([tw_real, tw_imag], 1).astype(jnp.bfloat16))
        spectra = lax.dot_general(
            second[...],
            jnp.concatenate(twisted, 0),
            (((1,), (1,)), ((), ())),
            preferred_element_type=jnp.float32,
        ).astype(jnp.bfloat16)
        for j in range(2):
            rows = pl.ds(pl.multiple_of((step * 2 + j) * CHUNK, CHUNK), CHUNK)
            for part in range(2):
                for group in range(CHANNELS // CHUNK):
                    start = part * CHANNELS + group * CHUNK
                    stage[group, rows, part * LANES : (part + 1) * LANES] = spectra[
                        start : start + CHUNK, j * LANES : (j + 1) * LANES
                    ]
        return carry

    lax.fori_loop(0, CHUNK // 2, pair, 0)

    def turn(group, carry):
        turned = jnp.dot(order[...], stage[group], preferred_element_type=jnp.float32)
        turned = turned.astype(jnp.bfloat16).reshape(CHUNK, CHUNK, 2 * LANES)
        out[k, pl.ds(group * CHUNK, CHUNK)] = turned
        return carry

    lax.fori_loop(0, CHANNELS // CHUNK, turn, 0)


def correlate(rows, columns, total, row_start, column_start):
    pieces = []
    for start in range(0, rows.shape[1], 2 * LANES):
        pieces.append(rows[:, start + LANES : start + 2 * LANES])
        pieces.append(-rows[:, start : start + LANES])
    flipped = jnp.concatenate(pieces, 1)
    contract = (((1,), (1,)), ((), ()))
    row_range = slice(row_start, row_start + rows.shape[0])
    column_range = slice(column_start, column_start + columns.shape[0])
    for part, left in enumerate((rows, flipped)):
        total[part, row_range, column_range] += lax.dot_general(
            left, columns, contract, preferred_element_type=jnp.float32
        )


def whole_kernel(
    volts,
    coeffs,
    first,
    second,
    order,
    cosine,
    sine,
    autos,
    cross,
    frames,
    stage,
    spectra,
    held,
    partial,
    outgoing,
    incoming,
    turn_send,
    turn_recv,
    halo_send,
    halo_recv,
    send_sem,
    recv_sem,
    cross_sem,
    pass_send,
    pass_recv,
    sum_sem,
    ready,
):
    me = lax.axis_index("inner")
    group = lax.axis_index("group")
    count = lax.axis_size("inner")
    other = 1 - group
    ring = lax.rem(me, RING)
    base = me - ring
    following = lax.rem(me + RING, count)
    tail = ring // (RING - HISTORY)
    zee = lax.rem(me // RING, ZS)
    ex = me // (RING * ZS)
    towards = 2 * group - 1
    plane = RING * XS
    chunks = spectra.shape[0]
    near = lax.rem(towards + ZS, ZS)
    far = lax.rem(ZS - towards, ZS)
    my_half = ex // (XS // 2)
    crossing = lax.rem(my_half + group, 2)
    staying = 1 - crossing
    met = lax.rem(my_half + other, 2)

    def at_distance(distance):
        return lax.rem(zee + distance + 2 * ZS, ZS)

    def place(step, zed):
        x_to = lax.rem(ex + step // RING, XS)
        ring_to = lax.rem(ring + lax.rem(step, RING), RING)
        return (x_to * ZS + zed) * RING + ring_to

    def to_half(half):
        def locate(step, zed):
            x_to = half * (XS // 2) + step // RING
            ring_to = lax.rem(ring + lax.rem(step, RING), RING)
            return (x_to * ZS + zed) * RING + ring_to

        return locate

    def x_lanes(x, width=1):
        return pl.ds(pl.multiple_of(x * 2 * LANES, 2 * LANES), width * 2 * LANES)

    def half_lanes(half):
        return x_lanes(half * (XS // 2), XS // 2)

    def arrived(ref, sem):
        pltpu.make_async_copy(ref, ref, sem).wait()

    barrier = pltpu.get_barrier_semaphore()
    blocks = count // RING

    def greet(group_to, begin):
        def body(step, carry):
            pl.semaphore_signal(
                barrier,
                inc=1,
                device_id={"group": group_to, "inner": lax.rem(me + step * RING, count)},
                device_id_type=MESH_ID,
            )
            return carry

        lax.fori_loop(begin, blocks, body, 0)

    mates = [base + lax.rem(ring + s, RING) for s in range(1, RING)]
    for mate in mates:
        pl.semaphore_signal(barrier, inc=1, device_id={"inner": mate}, device_id_type=MESH_ID)
    greet(group, 1)
    greet(other, 0)
    pl.semaphore_wait(barrier, 2 * blocks - 1 + RING - 1)

    def start_turn(k):
        mine = pl.ds(k * CHUNK, CHUNK)
        for s in range(1, RING):
            owner = lax.rem(ring + s, RING)
            pltpu.make_async_remote_copy(
                src_ref=volts.at[pl.ds((k * RING + owner) * CHUNK, CHUNK)],
                dst_ref=frames.at[HISTORY + ring, mine],
                send_sem=turn_send,
                recv_sem=turn_recv.at[k, tail],
                device_id={"inner": base + owner},
                device_id_type=MESH_ID,
            ).start()
        pltpu.make_async_copy(
            volts.at[pl.ds((k * RING + ring) * CHUNK, CHUNK)],
            frames.at[HISTORY + ring, mine],
            turn_recv.at[k, tail],
        ).start()

    def send_halo(k):
        mine = pl.ds(k * CHUNK, CHUNK)
        last = frames.at[pl.ds(RING, HISTORY), mine]
        arrived(last, turn_recv.at[k, 1])
        pltpu.make_async_remote_copy(
            src_ref=last,
            dst_ref=frames.at[pl.ds(0, HISTORY), mine],
            send_sem=halo_send,
            recv_sem=halo_recv.at[k],
            device_id={"inner": following},
            device_id_type=MESH_ID,
        ).start()

    def channelize(k):
        mine = pl.ds(k * CHUNK, CHUNK)
        arrived(frames.at[pl.ds(HISTORY, RING - HISTORY), mine], turn_recv.at[k, 0])
        arrived(frames.at[pl.ds(0, HISTORY), mine], halo_recv.at[k])

        @pl.when(me < RING)
        def _():
            frames[0:HISTORY, mine] = jnp.zeros(
                (HISTORY, CHUNK) + frames.shape[2:], frames.dtype
            )

        spectra_chunk(k, frames, coeffs, first, second, order, cosine, sine, stage, spectra)

    def send_spectra(k):
        row = k * RING + ring

        def send(group_to, zed, locate, begin, end, sem):
            slot = lax.rem(zee - zed + ZS, ZS)

            def body(step, carry):
                peer = locate(step, zed)
                pltpu.make_async_remote_copy(
                    src_ref=spectra.at[k, peer],
                    dst_ref=held.at[group, slot, row, :, x_lanes(ex)],
                    send_sem=send_sem,
                    recv_sem=sem(slot),
                    device_id={"group": group_to, "inner": peer},
                    device_id_type=MESH_ID,
                ).start()
                return carry

            lax.fori_loop(begin, end, body, 0)

        def by_slot(slot):
            return recv_sem.at[slot, k]

        def by_source(slot):
            return cross_sem.at[slot, k, ex]

        send(other, at_distance(towards), place, 0, plane, by_source)
        send(other, at_distance(2), to_half(crossing), 0, plane // 2, by_source)
        send(group, at_distance(2), to_half(staying), 0, plane // 2, by_slot)
        send(group, at_distance(-towards), place, 0, plane, by_slot)
        send(other, zee, to_half(crossing), 0, plane // 2, by_source)
        send(group, zee, place, 1, plane, by_slot)
        pltpu.make_async_copy(
            spectra.at[k, me], held.at[group, 0, row, :, x_lanes(ex)], recv_sem.at[0, k]
        ).start()

    def chunk_rows(k):
        return pl.ds(k * RING, RING)

    def hand_on(k):
        for x in range(XS):
            here = lax.rem(ex + XS - x, XS)
            pass_on(k, near, here, recv_sem.at[near, k])
        for x in range(XS // 2):
            pass_on(k, 2, met * (XS // 2) + x, pass_recv.at[k])

    def pass_on(k, slot, x, sem):
        block = held.at[other, slot, chunk_rows(k), :, x_lanes(x)]
        arrived(block, cross_sem.at[slot, k, x])
        pltpu.make_async_remote_copy(
            src_ref=block,
            dst_ref=block,
            send_sem=pass_send,
            recv_sem=sem,
            device_id={"group": other},
            device_id_type=MESH_ID,
        ).start()

    def flat(which, slot, begin, end, lanes=slice(None)):
        block = held[which, slot, begin * RING : end * RING, :, lanes]
        return block.reshape((end - begin) * RING * CHUNK, block.shape[-1])

    size = RING * CHUNK

    def add_early(which_rows, which_columns, slot, total, lanes=slice(None)):
        last = chunks - 1
        rows = flat(which_rows, slot, 0, last, lanes)
        columns = flat(which_columns, slot, 0, last, lanes)
        correlate(rows, columns, total, 0, 0)

    def add_late(which_rows, which_columns, slot, total, lanes=slice(None)):
        last = chunks - 1
        columns = flat(which_columns, slot, 0, chunks, lanes)
        correlate(flat(which_rows, slot, last, chunks, lanes), columns, total, last * size, 0)
        correlate(
            flat(which_rows, slot, 0, last, lanes), columns[last * size :], total, 0, last * size
        )

    def wait_own(slot, k):
        arrived(held.at[group, slot, chunk_rows(k)], recv_sem.at[slot, k])

    def wait_staying(k):
        arrived(held.at[group, 2, chunk_rows(k), :, half_lanes(met)], recv_sem.at[2, k])

    def wait_passed(k):
        arrived(held.at[group, 2, chunk_rows(k), :, half_lanes(1 - met)], pass_recv.at[k])

    def wait_level(k):
        for x in range(XS // 2):
            here = met * (XS // 2) + x
            arrived(
                held.at[other, 0, chunk_rows(k), :, x_lanes(here)], cross_sem.at[0, k, here]
            )

    for k in range(chunks):
        start_turn(k)
    for mate in mates:
        pl.semaphore_signal(ready, inc=1, device_id={"inner": mate}, device_id_type=MESH_ID)
    send_halo(0)
    send_halo(1)
    pl.semaphore_wait(ready, RING - 1)
    channelize(0)
    send_spectra(0)
    send_halo(2)
    channelize(1)
    send_spectra(1)
    hand_on(0)
    autos[...] = jnp.zeros(autos.shape, autos.dtype)
    partial[...] = jnp.zeros(partial.shape, partial.dtype)
    channelize(2)
    send_spectra(2)
    hand_on(1)
    for k in range(2):
        wait_own(0, k)
        wait_level(k)
    add_early(group, group, 0, autos)
    add_early(1, 0, 0, partial, half_lanes(met))
    hand_on(2)
    for k in range(2):
        wait_own(near, k)
    add_early(1, 0, near, partial)
    add_early(group, group, near, autos)
    for k in range(2):
        wait_staying(k)
    add_early(1, 0, 2, partial, half_lanes(met))
    for k in range(2):
        wait_passed(k)
    add_early(group, group, 2, autos)
    for k in range(2):
        wait_own(far, k)
    add_early(group, group, far, autos)
    wait_own(0, 2)
    wait_level(2)
    add_late(1, 0, 0, partial, half_lanes(met))
    wait_own(near, 2)
    add_late(1, 0, near, partial)
    wait_staying(2)
    add_late(1, 0, 2, partial, half_lanes(met))
    keep = chunks * size // 2
    theirs = partial[:, pl.ds(pl.multiple_of(other * keep, keep), keep)]
    outgoing[...] = theirs.astype(outgoing.dtype)
    swap = pltpu.make_async_remote_copy(
        src_ref=outgoing,
        dst_ref=incoming,
        send_sem=sum_sem.at[0],
        recv_sem=sum_sem.at[1],
        device_id={"group": other},
        device_id_type=MESH_ID,
    )
    swap.start()
    add_late(group, group, 0, autos)
    add_late(group, group, near, autos)
    wait_passed(2)
    add_late(group, group, 2, autos)
    wait_own(far, 2)
    add_late(group, group, far, autos)
    swap.wait()
    kept = partial[:, pl.ds(pl.multiple_of(group * keep, keep), keep)]
    cross[...] = kept + incoming[...].astype(jnp.float32)
    arrived(volts.at[pl.ds(0, (RING - 1) * chunks * CHUNK)], turn_send)
    arrived(frames.at[pl.ds(0, HISTORY)], halo_send)
    arrived(spectra.at[:, pl.ds(0, ZS * plane - 1)], send_sem)
    arrived(spectra.at[:, pl.ds(0, plane // 2)], send_sem)
    arrived(held.at[other, near], pass_send)
    arrived(held.at[other, 2, :, :, half_lanes(met)], pass_send)


def shards(voltages, coeffs):
    inputs = voltages.shape[1]
    volts = voltages.reshape(inputs, 2 * SUBCHANNELS, CHANNELS)
    chunks = inputs // (RING * CHUNK)
    vmem = pl.BlockSpec(memory_space=pltpu.VMEM)
    autos, cross = pl.pallas_call(
        whole_kernel,
        out_shape=(
            jax.ShapeDtypeStruct((2, inputs, inputs), jnp.float32),
            jax.ShapeDtypeStruct((2, inputs // 2, inputs), jnp.float32),
        ),
        in_specs=[pl.BlockSpec(memory_space=pl.ANY)] + [vmem] * 6,
        out_specs=(vmem, vmem),
        scratch_shapes=[
            pltpu.VMEM((RING + HISTORY, chunks * CHUNK) + volts.shape[1:], jnp.bfloat16),
            pltpu.VMEM((CHANNELS // CHUNK, CHUNK * CHUNK, 2 * LANES), jnp.bfloat16),
            pltpu.VMEM((chunks, CHANNELS, CHUNK, 2 * LANES), jnp.bfloat16),
            pltpu.VMEM((2, ZS, chunks * RING, CHUNK, XS * 2 * LANES), jnp.bfloat16),
            pltpu.VMEM((2, inputs, inputs), jnp.float32),
            pltpu.VMEM((2, inputs // 2, inputs), jnp.bfloat16),
            pltpu.VMEM((2, inputs // 2, inputs), jnp.bfloat16),
            pltpu.SemaphoreType.DMA,
            pltpu.SemaphoreType.DMA((chunks, 2)),
            pltpu.SemaphoreType.DMA,
            pltpu.SemaphoreType.DMA((chunks,)),
            pltpu.SemaphoreType.DMA,
            pltpu.SemaphoreType.DMA((ZS, chunks)),
            pltpu.SemaphoreType.DMA((ZS, chunks, XS)),
            pltpu.SemaphoreType.DMA,
            pltpu.SemaphoreType.DMA((chunks,)),
            pltpu.SemaphoreType.DMA((2,)),
            pltpu.SemaphoreType.REGULAR,
        ],
        compiler_params=pltpu.CompilerParams(collective_id=0, has_side_effects=True),
    )(volts, coeffs, *tables())
    scale = 1.0 / (RING * BLOCKS * SUBCHANNELS)
    return (autos[None] * scale, cross[None] * scale)


def solution(mesh):
    placed = (P("inner", "group", None, None, None), P())
    return jax.shard_map(
        shards,
        mesh=mesh,
        in_specs=placed,
        out_specs=(P("inner", None, "group", None), P("inner", None, "group", None)),
        check_vma=False,
    )
```

```python
import functools
import math

import jax
import jax.numpy as jnp
import numpy as np
from jax import lax
from jax.experimental import pallas as pl
from jax.experimental.pallas import tpu as pltpu
from jax.sharding import PartitionSpec as P

MESH_ID = pl.DeviceIdType.MESH
SUBCHANNELS = 16
TAPS = 3
CHANNELS = 128
RING = 8
BLOCKS = 16
ZS = 4
XS = 4
HISTORY = TAPS - 1
LANES = 128
CHUNK = 16


def dft_block(length_dft):
    indices = np.arange(length_dft)
    angles = 2.0 * np.pi * (indices[:, None] * indices[None, :] % length_dft) / length_dft
    cosine = np.cos(angles)
    sine_table = np.sin(angles)
    upper = np.stack([cosine, -sine_table], axis=1)
    lower = np.stack([sine_table, cosine], axis=1)
    return np.stack([upper, lower], axis=0)


def twiddle_tables(channel_count):
    fine_count = SUBCHANNELS * channel_count
    rows_k = np.arange(SUBCHANNELS)[:, None]
    cols_q = np.arange(channel_count)[None, :]
    angles = 2.0 * np.pi * (rows_k * cols_q % fine_count) / fine_count
    factor = 1.0 / math.sqrt(fine_count)
    return (np.cos(angles) * factor, np.sin(angles) * factor)


def tables():
    small = dft_block(SUBCHANNELS)
    first = np.einsum("fg,rpsk->sfkgrp", np.eye(RING), small)
    rows = RING * 2 * SUBCHANNELS
    first = first.reshape(rows, rows)
    second = dft_block(CHANNELS).reshape(2 * CHANNELS, 2 * CHANNELS).T
    order = np.einsum("ij,mn->mijn", np.eye(CHUNK), np.eye(CHUNK))
    order = order.reshape(CHUNK * CHUNK, CHUNK * CHUNK)
    cos_np, sin_np = twiddle_tables(CHANNELS)
    as_bf16 = [jnp.asarray(t, jnp.float32).astype(jnp.bfloat16) for t in (first, second, order)]
    as_f32 = [jnp.asarray(np.tile(t, (RING, 1)), jnp.float32) for t in (cos_np, sin_np)]
    return as_bf16 + as_f32


def spectra_chunk(k, frames, coeffs, first, second, order, cosine, sine, stage, out):
    half = CHANNELS
    taps = [jnp.concatenate([coeffs[t], coeffs[t]], 0) for t in range(TAPS)]

    def pair(step, carry):
        sections = []
        for j in range(2):
            source = k * CHUNK + step * 2 + j
            held = [frames[t, source].astype(jnp.float32) for t in range(RING + HISTORY)]
            rows = []
            for t in range(RING):
                total = taps[0] * held[t + HISTORY]
                for tap in range(1, TAPS):
                    total = total + taps[tap] * held[t + HISTORY - tap]
                rows.append(total.astype(jnp.bfloat16))
            sections.append(jnp.concatenate(rows, 0))
        filtered = jnp.concatenate(sections, 1)
        one = jnp.dot(first[...], filtered, preferred_element_type=jnp.float32)
        cos_tw = cosine[...]
        sin_tw = sine[...]
        twisted = []
        for j in range(2):
            lanes = slice(j * LANES, (j + 1) * LANES)
            real = one[:half, lanes]
            imag = one[half:, lanes]
            tw_real = real * cos_tw + imag * sin_tw
            tw_imag = imag * cos_tw - real * sin_tw
            twisted.append(jnp.concatenate([tw_real, tw_imag], 1).astype(jnp.bfloat16))
        spectra = lax.dot_general(
            second[...],
            jnp.concatenate(twisted, 0),
            (((1,), (1,)), ((), ())),
            preferred_element_type=jnp.float32,
        ).astype(jnp.bfloat16)
        for j in range(2):
            rows = pl.ds(pl.multiple_of((step * 2 + j) * CHUNK, CHUNK), CHUNK)
            for part in range(2):
                for group in range(CHANNELS // CHUNK):
                    start = part * CHANNELS + group * CHUNK
                    stage[group, rows, part * LANES : (part + 1) * LANES] = spectra[
                        start : start + CHUNK, j * LANES : (j + 1) * LANES
                    ]
        return carry

    lax.fori_loop(0, CHUNK // 2, pair, 0)

    def turn(group, carry):
        turned = jnp.dot(order[...], stage[group], preferred_element_type=jnp.float32)
        turned = turned.astype(jnp.bfloat16).reshape(CHUNK, CHUNK, 2 * LANES)
        out[k, pl.ds(group * CHUNK, CHUNK)] = turned
        return carry

    lax.fori_loop(0, CHANNELS // CHUNK, turn, 0)


def correlate(rows, columns, total, row_start, column_start):
    pieces = []
    for start in range(0, rows.shape[1], 2 * LANES):
        pieces.append(rows[:, start + LANES : start + 2 * LANES])
        pieces.append(-rows[:, start : start + LANES])
    flipped = jnp.concatenate(pieces, 1)
    contract = (((1,), (1,)), ((), ()))
    row_range = slice(row_start, row_start + rows.shape[0])
    column_range = slice(column_start, column_start + columns.shape[0])
    for part, left in enumerate((rows, flipped)):
        total[part, row_range, column_range] += lax.dot_general(
            left, columns, contract, preferred_element_type=jnp.float32
        )


def whole_kernel(
    volts,
    coeffs,
    first,
    second,
    order,
    cosine,
    sine,
    autos,
    cross,
    frames,
    stage,
    spectra,
    held,
    partial,
    outgoing,
    incoming,
    turn_send,
    turn_recv,
    halo_send,
    halo_recv,
    send_sem,
    recv_sem,
    cross_sem,
    pass_send,
    pass_recv,
    sum_sem,
    ready,
):
    me = lax.axis_index("inner")
    group = lax.axis_index("group")
    count = lax.axis_size("inner")
    other = 1 - group
    ring = lax.rem(me, RING)
    base = me - ring
    following = lax.rem(me + RING, count)
    tail = ring // (RING - HISTORY)
    zee = lax.rem(me // RING, ZS)
    ex = me // (RING * ZS)
    towards = 2 * group - 1
    plane = RING * XS
    chunks = spectra.shape[0]
    near = lax.rem(towards + ZS, ZS)
    far = lax.rem(ZS - towards, ZS)
    my_half = ex // (XS // 2)
    crossing = lax.rem(my_half + group, 2)
    staying = 1 - crossing
    met = lax.rem(my_half + other, 2)

    def at_distance(distance):
        return lax.rem(zee + distance + 2 * ZS, ZS)

    def place(step, zed):
        x_to = lax.rem(ex + step // RING, XS)
        ring_to = lax.rem(ring + lax.rem(step, RING), RING)
        return (x_to * ZS + zed) * RING + ring_to

    def to_half(half):
        def locate(step, zed):
            x_to = half * (XS // 2) + step // RING
            ring_to = lax.rem(ring + lax.rem(step, RING), RING)
            return (x_to * ZS + zed) * RING + ring_to

        return locate

    def x_lanes(x, width=1):
        return pl.ds(pl.multiple_of(x * 2 * LANES, 2 * LANES), width * 2 * LANES)

    def half_lanes(half):
        return x_lanes(half * (XS // 2), XS // 2)

    def arrived(ref, sem):
        pltpu.make_async_copy(ref, ref, sem).wait()

    barrier = pltpu.get_barrier_semaphore()
    blocks = count // RING

    def greet(group_to, begin):
        def body(step, carry):
            pl.semaphore_signal(
                barrier,
                inc=1,
                device_id={"group": group_to, "inner": lax.rem(me + step * RING, count)},
                device_id_type=MESH_ID,
            )
            return carry

        lax.fori_loop(begin, blocks, body, 0)

    mates = [base + lax.rem(ring + s, RING) for s in range(1, RING)]
    for mate in mates:
        pl.semaphore_signal(barrier, inc=1, device_id={"inner": mate}, device_id_type=MESH_ID)
    greet(group, 1)
    greet(other, 0)
    pl.semaphore_wait(barrier, 2 * blocks - 1 + RING - 1)

    def start_turn(k):
        mine = pl.ds(k * CHUNK, CHUNK)
        for s in range(1, RING):
            owner = lax.rem(ring + s, RING)
            pltpu.make_async_remote_copy(
                src_ref=volts.at[pl.ds((k * RING + owner) * CHUNK, CHUNK)],
                dst_ref=frames.at[HISTORY + ring, mine],
                send_sem=turn_send,
                recv_sem=turn_recv.at[k, tail],
                device_id={"inner": base + owner},
                device_id_type=MESH_ID,
            ).start()
        pltpu.make_async_copy(
            volts.at[pl.ds((k * RING + ring) * CHUNK, CHUNK)],
            frames.at[HISTORY + ring, mine],
            turn_recv.at[k, tail],
        ).start()

    def send_halo(k):
        mine = pl.ds(k * CHUNK, CHUNK)
        last = frames.at[pl.ds(RING, HISTORY), mine]
        arrived(last, turn_recv.at[k, 1])
        pltpu.make_async_remote_copy(
            src_ref=last,
            dst_ref=frames.at[pl.ds(0, HISTORY), mine],
            send_sem=halo_send,
            recv_sem=halo_recv.at[k],
            device_id={"inner": following},
            device_id_type=MESH_ID,
        ).start()

    def channelize(k):
        mine = pl.ds(k * CHUNK, CHUNK)
        arrived(frames.at[pl.ds(HISTORY, RING - HISTORY), mine], turn_recv.at[k, 0])
        arrived(frames.at[pl.ds(0, HISTORY), mine], halo_recv.at[k])

        @pl.when(me < RING)
        def _():
            frames[0:HISTORY, mine] = jnp.zeros(
                (HISTORY, CHUNK) + frames.shape[2:], frames.dtype
            )

        spectra_chunk(k, frames, coeffs, first, second, order, cosine, sine, stage, spectra)

    def send_spectra(k):
        row = k * RING + ring

        def send(group_to, zed, locate, begin, end, sem):
            slot = lax.rem(zee - zed + ZS, ZS)

            def body(step, carry):
                peer = locate(step, zed)
                pltpu.make_async_remote_copy(
                    src_ref=spectra.at[k, peer],
                    dst_ref=held.at[group, slot, row, :, x_lanes(ex)],
                    send_sem=send_sem,
                    recv_sem=sem(slot),
                    device_id={"group": group_to, "inner": peer},
                    device_id_type=MESH_ID,
                ).start()
                return carry

            lax.fori_loop(begin, end, body, 0)

        def by_slot(slot):
            return recv_sem.at[slot, k]

        def by_source(slot):
            return cross_sem.at[slot, k, ex]

        send(other, at_distance(towards), place, 0, plane, by_source)
        send(other, at_distance(2), to_half(crossing), 0, plane // 2, by_source)
        send(group, at_distance(2), to_half(staying), 0, plane // 2, by_slot)
        send(group, at_distance(-towards), place, 0, plane, by_slot)
        send(other, zee, to_half(crossing), 0, plane // 2, by_source)
        send(group, zee, place, 1, plane, by_slot)
        pltpu.make_async_copy(
            spectra.at[k, me], held.at[group, 0, row, :, x_lanes(ex)], recv_sem.at[0, k]
        ).start()

    def chunk_rows(k):
        return pl.ds(k * RING, RING)

    def hand_on(k):
        for x in range(XS):
            here = lax.rem(ex + XS - x, XS)
            pass_on(k, near, here, recv_sem.at[near, k])
        for x in range(XS // 2):
            pass_on(k, 2, met * (XS // 2) + x, pass_recv.at[k])

    def pass_on(k, slot, x, sem):
        block = held.at[other, slot, chunk_rows(k), :, x_lanes(x)]
        arrived(block, cross_sem.at[slot, k, x])
        pltpu.make_async_remote_copy(
            src_ref=block,
            dst_ref=block,
            send_sem=pass_send,
            recv_sem=sem,
            device_id={"group": other},
            device_id_type=MESH_ID,
        ).start()

    def flat(which, slot, begin, end, lanes=slice(None)):
        block = held[which, slot, begin * RING : end * RING, :, lanes]
        return block.reshape((end - begin) * RING * CHUNK, block.shape[-1])

    size = RING * CHUNK

    def add_early(which_rows, which_columns, slot, total, lanes=slice(None)):
        last = chunks - 1
        rows = flat(which_rows, slot, 0, last, lanes)
        columns = flat(which_columns, slot, 0, last, lanes)
        correlate(rows, columns, total, 0, 0)

    def add_late(which_rows, which_columns, slot, total, lanes=slice(None)):
        last = chunks - 1
        columns = flat(which_columns, slot, 0, chunks, lanes)
        correlate(flat(which_rows, slot, last, chunks, lanes), columns, total, last * size, 0)
        correlate(
            flat(which_rows, slot, 0, last, lanes), columns[last * size :], total, 0, last * size
        )

    def wait_own(slot, k):
        arrived(held.at[group, slot, chunk_rows(k)], recv_sem.at[slot, k])

    def wait_staying(k):
        arrived(held.at[group, 2, chunk_rows(k), :, half_lanes(met)], recv_sem.at[2, k])

    def wait_passed(k):
        arrived(held.at[group, 2, chunk_rows(k), :, half_lanes(1 - met)], pass_recv.at[k])

    def wait_level(k):
        for x in range(XS // 2):
            here = met * (XS // 2) + x
            arrived(
                held.at[other, 0, chunk_rows(k), :, x_lanes(here)], cross_sem.at[0, k, here]
            )

    for k in range(chunks):
        start_turn(k)
    for mate in mates:
        pl.semaphore_signal(ready, inc=1, device_id={"inner": mate}, device_id_type=MESH_ID)
    send_halo(0)
    send_halo(1)
    pl.semaphore_wait(ready, RING - 1)
    channelize(0)
    send_spectra(0)
    send_halo(2)
    channelize(1)
    send_spectra(1)
    hand_on(0)
    autos[...] = jnp.zeros(autos.shape, autos.dtype)
    partial[...] = jnp.zeros(partial.shape, partial.dtype)
    channelize(2)
    send_spectra(2)
    hand_on(1)
    hand_on(2)
    for k in range(2):
        wait_own(0, k)
        wait_level(k)
    add_early(group, group, 0, autos)
    add_early(1, 0, 0, partial, half_lanes(met))
    for k in range(2):
        wait_own(near, k)
    add_early(1, 0, near, partial)
    add_early(group, group, near, autos)
    for k in range(2):
        wait_staying(k)
    add_early(1, 0, 2, partial, half_lanes(met))
    for k in range(2):
        wait_passed(k)
    add_early(group, group, 2, autos)
    for k in range(2):
        wait_own(far, k)
    add_early(group, group, far, autos)
    wait_own(0, 2)
    wait_level(2)
    add_late(1, 0, 0, partial, half_lanes(met))
    wait_own(near, 2)
    add_late(1, 0, near, partial)
    wait_staying(2)
    add_late(1, 0, 2, partial, half_lanes(met))
    keep = chunks * size // 2
    theirs = partial[:, pl.ds(pl.multiple_of(other * keep, keep), keep)]
    outgoing[...] = theirs.astype(outgoing.dtype)
    swap = pltpu.make_async_remote_copy(
        src_ref=outgoing,
        dst_ref=incoming,
        send_sem=sum_sem.at[0],
        recv_sem=sum_sem.at[1],
        device_id={"group": other},
        device_id_type=MESH_ID,
    )
    swap.start()
    add_late(group, group, 0, autos)
    add_late(group, group, near, autos)
    wait_passed(2)
    add_late(group, group, 2, autos)
    wait_own(far, 2)
    add_late(group, group, far, autos)
    swap.wait()
    kept = partial[:, pl.ds(pl.multiple_of(group * keep, keep), keep)]
    cross[...] = kept + incoming[...].astype(jnp.float32)
    arrived(volts.at[pl.ds(0, (RING - 1) * chunks * CHUNK)], turn_send)
    arrived(frames.at[pl.ds(0, HISTORY)], halo_send)
    arrived(spectra.at[:, pl.ds(0, ZS * plane - 1)], send_sem)
    arrived(spectra.at[:, pl.ds(0, plane // 2)], send_sem)
    arrived(held.at[other, near], pass_send)
    arrived(held.at[other, 2, :, :, half_lanes(met)], pass_send)


def shards(voltages, coeffs):
    inputs = voltages.shape[1]
    volts = voltages.reshape(inputs, 2 * SUBCHANNELS, CHANNELS)
    chunks = inputs // (RING * CHUNK)
    vmem = pl.BlockSpec(memory_space=pltpu.VMEM)
    autos, cross = pl.pallas_call(
        whole_kernel,
        out_shape=(
            jax.ShapeDtypeStruct((2, inputs, inputs), jnp.float32),
            jax.ShapeDtypeStruct((2, inputs // 2, inputs), jnp.float32),
        ),
        in_specs=[pl.BlockSpec(memory_space=pl.ANY)] + [vmem] * 6,
        out_specs=(vmem, vmem),
        scratch_shapes=[
            pltpu.VMEM((RING + HISTORY, chunks * CHUNK) + volts.shape[1:], jnp.bfloat16),
            pltpu.VMEM((CHANNELS // CHUNK, CHUNK * CHUNK, 2 * LANES), jnp.bfloat16),
            pltpu.VMEM((chunks, CHANNELS, CHUNK, 2 * LANES), jnp.bfloat16),
            pltpu.VMEM((2, ZS, chunks * RING, CHUNK, XS * 2 * LANES), jnp.bfloat16),
            pltpu.VMEM((2, inputs, inputs), jnp.float32),
            pltpu.VMEM((2, inputs // 2, inputs), jnp.bfloat16),
            pltpu.VMEM((2, inputs // 2, inputs), jnp.bfloat16),
            pltpu.SemaphoreType.DMA,
            pltpu.SemaphoreType.DMA((chunks, 2)),
            pltpu.SemaphoreType.DMA,
            pltpu.SemaphoreType.DMA((chunks,)),
            pltpu.SemaphoreType.DMA,
            pltpu.SemaphoreType.DMA((ZS, chunks)),
            pltpu.SemaphoreType.DMA((ZS, chunks, XS)),
            pltpu.SemaphoreType.DMA,
            pltpu.SemaphoreType.DMA((chunks,)),
            pltpu.SemaphoreType.DMA((2,)),
            pltpu.SemaphoreType.REGULAR,
        ],
        compiler_params=pltpu.CompilerParams(collective_id=0, has_side_effects=True),
    )(volts, coeffs, *tables())
    scale = 1.0 / (RING * BLOCKS * SUBCHANNELS)
    return (autos[None] * scale, cross[None] * scale)


def solution(mesh):
    placed = (P("inner", "group", None, None, None), P())
    return jax.shard_map(
        shards,
        mesh=mesh,
        in_specs=placed,
        out_specs=(P("inner", None, "group", None), P("inner", None, "group", None)),
        check_vma=False,
    )
```
